32 devices in a mesh: batch: 8 (over z, core), seq: 4 (over y, x).
Axes of the slice: x: 2, y: 2, z: 4, core: 2. Of those that a mesh axis runs over, the one named last changes fastest.
Arguments:
- tokens: bfloat16 [16, 1024, 1152], P('batch', 'seq')
- prefix_len: int32 [16], P('batch'), may hold values from 102 to 512
- attention_gain: float32 [1152], replicated, may hold values from 0.1 to 1.9
- query_weight: bfloat16 [1152, 1152], P('batch', 'seq'), may hold values from -0.1875 to 0.1875
- key_weight: bfloat16 [1152, 384], P('batch', 'seq'), may hold values from -0.1875 to 0.1875
- value_weight: bfloat16 [1152, 384], P('batch', 'seq'), may hold values from -0.1875 to 0.1875
- output_weight: bfloat16 [1152, 1152], P('batch', 'seq'), may hold values from -4 to 4
- mlp_gain: float32 [1152], replicated, may hold values from 0.1 to 1.9
- gate_weight: bfloat16 [1152, 3072], P('batch', 'seq'), may hold values from -0.1875 to 0.1875
- up_weight: bfloat16 [1152, 3072], P('batch', 'seq'), may hold values from -0.1875 to 0.1875
- down_weight: bfloat16 [3072, 1152], P('batch', 'seq'), may hold values from -0.109375 to 0.109375
- cotangent: bfloat16 [16, 1024, 1152], P('batch', 'seq'), may hold values from -6 to 6
Outputs:
- layer_output: bfloat16 [16, 1024, 1152], P('batch', 'seq')
- input_grad: float32 [16, 1024, 1152], P('batch', 'seq')
- attention_gain_grad: float32 [1152], replicated
- query_grad: float32 [1152, 1152], P('batch', 'seq')
- key_grad: float32 [1152, 384], P('batch', 'seq')
- value_grad: float32 [1152, 384], P('batch', 'seq')
- output_grad: float32 [1152, 1152], P('batch', 'seq')
- mlp_gain_grad: float32 [1152], replicated
- gate_grad: float32 [1152, 3072], P('batch', 'seq')
- up_grad: float32 [1152, 3072], P('batch', 'seq')
- down_weight_gradient: float32 [3072, 1152], P('batch', 'seq')
- residual_rms: float32 [3], replicated
The draws below stay inside these ranges and needn't reach their ends.
All inputs are finite; a program needn't handle non-finite values.
Results may differ from the reference program's by a relative error of at most 0.02.
Values may be sent and summed in bfloat16 or wider, within the bound.
No kernel may reach another device: no remote copies, remote signals or barrier semaphores. Data moves between devices by JAX's collectives and lax.ppermute only.
A program may use at most 192 MiB of HBM per device.

```python
import jax
import jax.numpy as jnp
from jax import lax

D = 1152
HEADS = 18
KV_HEADS = 6
HEAD = 64
FF = 3072
SEQ_LEN = 1024
SEQS = 16


def draw_tokens(key, part):
    first, second, third = jax.random.split(key, 3)
    shape = (SEQS, SEQ_LEN, D)
    base = jax.random.normal(first, shape, jnp.float32)
    position = jnp.arange(SEQS, dtype=jnp.float32)[:, None] * SEQ_LEN + jnp.arange(SEQ_LEN, dtype=jnp.float32)[None, :]
    ramp = 1.0 + 2.0 * position / (SEQS * SEQ_LEN - 1.0)
    row_scale = jnp.exp(jax.random.uniform(second, (SEQS, SEQ_LEN, 1), jnp.float32, -0.7, 0.7))
    column_scale = jnp.exp(jax.random.uniform(third, (1, 1, D), jnp.float32, -0.7, 0.7))
    return (base * ramp[:, :, None] * row_scale * column_scale).astype(jnp.bfloat16)


def set_ends(result, stream_key, low, top_value):
    extent = result.shape
    spot = [jax.random.randint(jax.random.fold_in(stream_key, axis), (), 0, extent[axis]) for axis in range(len(extent))]
    result = result.at[tuple(spot)].set(low)
    longest = extent.index(max(extent))
    spot[longest] = (spot[longest] + 1) % extent[longest]
    return result.at[tuple(spot)].set(top_value)


def steps_of(key, dims, cuts, low, top_value):
    factor_of = 1.0
    for dim, shards_of in cuts:
        draws = jax.random.uniform(jax.random.fold_in(jax.random.fold_in(key, 6), dim), (shards_of,), jnp.float32, low / len(cuts), top_value / len(cuts))
        factor_of = factor_of * jnp.repeat(jnp.exp(draws), dims[dim] // shards_of).reshape((-1,) + (1,) * (len(dims) - 1 - dim))
    return factor_of


def noise(rng, extent, scale, reach, cuts=(), kind=jnp.bfloat16):
    result = scale * jax.random.normal(rng, extent, jnp.float32)
    if cuts:
        result = result * steps_of(rng, extent, cuts, -0.22, 0.18)
    return jnp.clip(result, -reach, reach).astype(kind)


def setup_inputs(seed: int = 0) -> dict:
    key_list = jax.random.split(jax.random.key(seed), 13)
    return {
        "tokens": draw_tokens(jax.random.fold_in(key_list[12], 71), 0),
        "prefix_len": set_ends(jax.random.randint(key_list[1], (SEQS,), SEQ_LEN // 10, SEQ_LEN // 2 + 1), jax.random.fold_in(key_list[1], 1), SEQ_LEN // 10, (SEQ_LEN // 2 + 1) - 1).astype(jnp.int32),
        "attention_gain": jnp.clip(1.0 + 0.18 * jax.random.normal(key_list[2], (D,), jnp.float32), 0.1, 1.9),
        "query_weight": noise(key_list[3], (D, D), D ** -0.5, 0.1875, ((0, 8), (1, 4))),
        "key_weight": noise(key_list[4], (D, KV_HEADS * HEAD), D ** -0.5, 0.1875, ((0, 8), (1, 4))),
        "value_weight": noise(key_list[5], (D, KV_HEADS * HEAD), D ** -0.5, 0.1875, ((0, 8), (1, 4))),
        "output_weight": noise(key_list[6], (D, D), (max(1, D // 512)) ** -0.5, 4.0, ((0, 8), (1, 4))),
        "mlp_gain": jnp.clip(1.0 + 0.18 * jax.random.normal(key_list[7], (D,), jnp.float32), 0.1, 1.9),
        "gate_weight": noise(key_list[8], (D, FF), D ** -0.5, 0.1875, ((0, 8), (1, 4))),
        "up_weight": noise(key_list[9], (D, FF), D ** -0.5, 0.1875, ((0, 8), (1, 4))),
        "down_weight": noise(key_list[10], (FF, D), FF ** -0.5, 0.109375, ((0, 8), (1, 4))),
        "cotangent": noise(key_list[11], (SEQS, SEQ_LEN, D), 1.0, 6.0, ((0, 8), (1, 4))),
    }


EPSILON = 1e-05
MASKED = -1e+30
HIGHEST = lax.Precision.HIGHEST

@jax.custom_vjp
def low(v):
    return lax.optimization_barrier(v.astype(jnp.bfloat16)).astype(jnp.float32)

@jax.custom_vjp
def low_back(v):
    return v

def low_keep(v):
    return (low(v), None)

def low_pass(kept, grad):
    return (grad,)

def back_keep(v):
    return (v, None)

def back_low(kept, grad):
    return (low(grad),)
low.defvjp(low_keep, low_pass)
low_back.defvjp(back_keep, back_low)

def rope_tables(positions, half_width):
    frequency = 10000.0 ** (-(jnp.arange(half_width, dtype=jnp.float32) * 2.0) / (2.0 * half_width))
    angles = positions.astype(jnp.float32)[:, None] * frequency[None, :]
    return (jnp.cos(angles)[:, None, :], jnp.sin(angles)[:, None, :])

def rotate(values, cosine, sine):
    half_width = values.shape[-1] // 2
    former = values[..., :half_width]
    trailing_operand = values[..., half_width:]
    return jnp.concatenate([former * cosine - trailing_operand * sine, trailing_operand * cosine + former * sine], -1)

def matmul(left_operand, right_operand):
    return jnp.einsum('bld,de->ble', left_operand, right_operand, precision=HIGHEST)

def attention_sequence(packed):
    queries, keys, values, prefix = packed
    block = min(512, SEQ_LEN)
    blocks = SEQ_LEN // block
    groups = HEADS // KV_HEADS
    grouped = queries.reshape(blocks, block, KV_HEADS, groups, HEAD)
    starts = jnp.arange(blocks, dtype=jnp.int32) * block
    key_position = jnp.arange(SEQ_LEN, dtype=jnp.int32)

    def query_block(item):
        chosen, start = item
        scores = jnp.einsum('lhgd,khd->hglk', chosen, keys, precision=HIGHEST) * HEAD ** (-0.5)
        scores = low_back(scores)
        row_position = start + jnp.arange(block, dtype=jnp.int32)
        visible = (key_position[None, :] <= row_position[:, None]) | (key_position[None, :] < prefix)
        scores = jnp.where(visible[None, None], scores, MASKED)
        weights = low(jax.nn.softmax(scores, axis=-1))
        return jnp.einsum('hglk,khd->lhgd', weights, values, precision=HIGHEST)
    mixed = lax.map(jax.checkpoint(query_block), (grouped, starts))
    return mixed.reshape(SEQ_LEN, HEADS * HEAD)

def layer_forward(params, inputs, prefixes, cosine, sine):
    gain_a, w_query, w_key, w_value, w_output, gain_m, w_gate, w_up, w_down = params
    batch_seqs = inputs.shape[0]
    inverse_a = lax.rsqrt(lax.optimization_barrier(jnp.mean(inputs * inputs, -1, keepdims=True)) + EPSILON)
    normed_a = low(inputs * inverse_a * gain_a)
    query_pre = low_back(matmul(normed_a, w_query))
    key_pre = low_back(matmul(normed_a, w_key))
    values = low_back(low(matmul(normed_a, w_value)))
    queries = low(rotate(query_pre.reshape(batch_seqs, SEQ_LEN, HEADS, HEAD), cosine, sine))
    keys = low(rotate(key_pre.reshape(batch_seqs, SEQ_LEN, KV_HEADS, HEAD), cosine, sine))
    values = values.reshape(batch_seqs, SEQ_LEN, KV_HEADS, HEAD)
    mixed = lax.map(attention_sequence, (queries, keys, values, prefixes))
    mixed = low(low_back(mixed))
    attn_branch = low_back(matmul(mixed, w_output))
    middle = inputs + attn_branch
    inverse_m = lax.rsqrt(lax.optimization_barrier(jnp.mean(middle * middle, -1, keepdims=True)) + EPSILON)
    normed_m = low(middle * inverse_m * gain_m)
    gate = low_back(matmul(normed_m, w_gate))
    upper = low_back(matmul(normed_m, w_up))
    hidden = low(jax.nn.silu(gate) * upper)
    mlp_branch = low_back(matmul(hidden, w_down))
    return (middle + mlp_branch, (attn_branch, mlp_branch))

def group_size():
    limit = max(1, 4096 // SEQ_LEN)
    chosen = 1
    for candidate in range(1, limit + 1):
        if SEQS % candidate == 0:
            chosen = candidate
    return chosen

def reference(tokens, prefix_len, attention_gain, query_weight, key_weight, value_weight, output_weight, mlp_gain, gate_weight, up_weight, down_weight, cotangent):
    params = (attention_gain.astype(jnp.float32), query_weight.astype(jnp.float32), key_weight.astype(jnp.float32), value_weight.astype(jnp.float32), output_weight.astype(jnp.float32), mlp_gain.astype(jnp.float32), gate_weight.astype(jnp.float32), up_weight.astype(jnp.float32), down_weight.astype(jnp.float32))
    group = group_size()
    steps_count = SEQS // group
    inputs = tokens.astype(jnp.float32).reshape(steps_count, group, SEQ_LEN, D)
    upstream = cotangent.astype(jnp.float32).reshape(steps_count, group, SEQ_LEN, D)
    prefixes = prefix_len.astype(jnp.int32).reshape(steps_count, group)
    cosine, sine = rope_tables(jnp.arange(SEQ_LEN, dtype=jnp.int32), HEAD // 2)

    def scan_step(carry, item):
        grads, sums = carry
        stretch_in, stretch_up, stretch_prefix = item

        def forward(weights, values):
            return layer_forward(weights, values, stretch_prefix, cosine, sine)
        output, pullback, branches = jax.vjp(forward, params, stretch_in, has_aux=True)
        param_grads, input_grads = pullback(stretch_up)
        attn_branch, mlp_branch = branches
        sums = sums + jnp.stack([jnp.sum(stretch_in * stretch_in), jnp.sum(attn_branch * attn_branch), jnp.sum(mlp_branch * mlp_branch)])
        grads = jax.tree.map(lambda total, extra: total + extra, grads, param_grads)
        return ((grads, sums), (output.astype(jnp.bfloat16), input_grads))
    initial = (jax.tree.map(jnp.zeros_like, params), jnp.zeros((3,), jnp.float32))
    (grads, sums), (outputs, input_grads) = lax.scan(scan_step, initial, (inputs, upstream, prefixes))
    residual_rms = jnp.sqrt(sums / (SEQS * SEQ_LEN * D))
    return (outputs.reshape(SEQS, SEQ_LEN, D), input_grads.reshape(SEQS, SEQ_LEN, D), grads[0], grads[1], grads[2], grads[3], grads[4], grads[5], grads[6], grads[7], grads[8], residual_rms)
```

```python
import functools
import math

import jax
import jax.numpy as jnp
from jax import lax
from jax.experimental import pallas as pl
from jax.experimental.pallas import tpu as pltpu
from jax.sharding import PartitionSpec as P

HEADS = 18
KV_HEADS = 6
HEAD = 64
SEQ_LEN = 1024
GROUP = HEADS // KV_HEADS
PAIRS = KV_HEADS // 2
EPSILON = 1e-05
MASKED = -1e30
SCALE = HEAD ** (-0.5)
F32 = jnp.float32
BF16 = jnp.bfloat16


def dot(a, b, ca=1, cb=0):
    return lax.dot_general(a, b, (((ca,), (cb,)), ((), ())), preferred_element_type=F32)


def whole(shape, **kw):
    zeros = (0,) * len(shape)
    return pl.BlockSpec(shape, lambda *_: zeros, **kw)


def once(shape):
    return whole(shape, pipeline_mode=pl.Buffered(1))


def call(body, grid, scalars, in_specs, out_specs, out_shape, scratch, args, name):
    return pl.pallas_call(
        body,
        grid_spec=pltpu.PrefetchScalarGridSpec(
            num_scalar_prefetch=len(scalars),
            grid=grid,
            in_specs=in_specs,
            out_specs=out_specs,
            scratch_shapes=scratch,
        ),
        out_shape=out_shape,
        compiler_params=pltpu.CompilerParams(
            dimension_semantics=("arbitrary",) * len(grid), vmem_limit_bytes=60 * 2**20
        ),
        name=name,
    )(*scalars, *args)


def shape(dims, kind=BF16):
    return jax.ShapeDtypeStruct(dims, kind)


def swap_halves(v):
    lane = lax.broadcasted_iota(jnp.int32, v.shape, 1) % HEAD
    n = v.shape[1]
    return jnp.where(lane < HEAD // 2, pltpu.roll(v, n - HEAD // 2, 1), pltpu.roll(v, HEAD // 2, 1))


def turn(v, cosine, sine):
    width = cosine.shape[1]
    parts = []
    for j in range(v.shape[1] // width):
        u = v[:, j * width : (j + 1) * width]
        parts.append(u * cosine + swap_halves(u) * sine)
    return jnp.concatenate(parts, 1)


def split_rows(value, nz):
    rows = value.shape[0] // (2 * nz)
    take = lambda c: jnp.concatenate(
        [value[(2 * z + c) * rows : (2 * z + c + 1) * rows] for z in range(nz)], 0
    )
    return take(0), take(1)


def split_lanes(value, nz):
    cols = value.shape[1] // (2 * nz)
    take = lambda c: jnp.concatenate(
        [value[:, (2 * z + c) * cols : (2 * z + c + 1) * cols] for z in range(nz)], 1
    )
    return take(0), take(1)


def ceil_lanes(n):
    return -(-n // 128) * 128


def project(tokens, gain, cosine, sine, blocks, where, nz):
    t, d = tokens.shape
    _, rows, wide = blocks[0].shape
    ns, nb = len(blocks) // 2, 2 * nz
    kv = KV_HEADS * HEAD
    qw, kw = d // ns, kv // ns

    def body(at, tok, gn, cs, sn, *refs):
        parts, (w, nt, q, k, v, q_s, k_s, v_s) = refs[: 2 * ns], refs[2 * ns :]
        for p in range(ns):
            for c in range(2):
                for z in range(nz):
                    w[at[p], at[ns + c * nz + z]] = parts[c * ns + p][z]
        x = tok[...].astype(F32)
        r = lax.rsqrt(jnp.mean(x * x, -1, keepdims=True) + EPSILON)
        n = (x * r * gn[...]).astype(BF16)
        a, b = split_rows(n.T, nz)
        nt[0] = a
        nt[1] = b
        for i in range(ns):
            weight = jnp.concatenate([w[i, j] for j in range(nb)], 0)
            y = dot(n, weight)
            q_s[:, i * qw : (i + 1) * qw] = y[:, :qw]
            k_s[:, i * kw : (i + 1) * kw] = y[:, qw : qw + kw]
            v_s[:, i * kw : (i + 1) * kw] = y[:, qw + kw : qw + 2 * kw]
        q[...] = turn(q_s[...], cs[...], sn[...]).astype(BF16)
        k[...] = turn(k_s[...], cs[...], sn[...]).astype(BF16)
        v[...] = v_s[...].astype(BF16)

    return call(
        body,
        (1,),
        (where,),
        [once((t, d)), once((1, d)), once(cosine.shape), once(sine.shape)] + [once(v.shape) for v in blocks],
        [whole((ns, nb, rows, wide)), whole((2, d // 2, t)), whole((t, d)), whole((t, kv)), whole((t, kv))],
        [shape((ns, nb, rows, wide)), shape((2, d // 2, t)), shape((t, d)), shape((t, kv)), shape((t, kv))],
        [pltpu.VMEM((t, d), F32), pltpu.VMEM((t, kv), F32), pltpu.VMEM((t, kv), F32)],
        (tokens, gain, cosine, sine, *blocks),
        "project",
    )


def fill_bias(meta, bias, ns, length):
    b = pl.program_id(0)
    prefix = meta[1 + ns + b]
    for i in range(ns):
        key = meta[1 + i] + lax.broadcasted_iota(jnp.int32, (length, length), 0)
        row = meta[0] + lax.broadcasted_iota(jnp.int32, (length, length), 1)
        bias[i * length : (i + 1) * length, :] = jnp.where(
            (key <= row) | (key < prefix), 0.0, MASKED
        ).astype(F32)


def key_rows(refs, lanes, side, first_major):
    parts = []
    for i in range(side):
        for j in range(side):
            ref = refs[i] if first_major else refs[j]
            parts.append(ref[j if first_major else i, :, lanes])
    return jnp.concatenate(parts, 0)


def attend(q, keys, values, meta, seqs, length):
    t, d = q.shape
    side = len(keys)
    ns = side * side
    kv = KV_HEADS * HEAD

    def body(meta, *refs):
        qr, kr, vr = refs[0], refs[1 : 1 + side], refs[1 + side : 1 + 2 * side]
        out, lse, bias = refs[1 + 2 * side :]
        fill_bias(meta, bias, ns, length)

        def pair(p, _):
            wide = pl.ds(pl.multiple_of(p * 2 * GROUP * HEAD, 128), 2 * GROUP * HEAD)
            narrow = pl.ds(pl.multiple_of(p * 2 * HEAD, 128), 2 * HEAD)
            qp = qr[:, wide]
            kp = key_rows(kr, narrow, side, True)
            vp = key_rows(vr, narrow, side, False)
            outs = []
            for g in range(2):
                k = kp[:, g * HEAD : (g + 1) * HEAD]
                vt = vp[:, g * HEAD : (g + 1) * HEAD].T
                for h in range(GROUP):
                    i = g * GROUP + h
                    one = qp[:, i * HEAD : (i + 1) * HEAD] * jnp.asarray(SCALE, BF16)
                    score = dot(k, one, 1, 1) + bias[...]
                    top = jnp.max(score, 0, keepdims=True)
                    e = jnp.exp(score - top)
                    total = jnp.sum(e, 0, keepdims=True)
                    outs.append(dot(vt, e.astype(BF16)) * (1.0 / total))
                    lse[0, p, pl.ds(i, 1), :] = top + jnp.log(total)
            out[:, wide] = jnp.concatenate(outs, 0).T.astype(BF16)
            return 0

        lax.fori_loop(0, PAIRS, pair, 0)

    kv_spec = pl.BlockSpec((side, length, kv), lambda b, m: (0, b, 0))
    row = pl.BlockSpec((length, d), lambda b, m: (b, 0))
    return call(
        body,
        (seqs,),
        (meta,),
        [row] + [kv_spec] * (2 * side),
        [row, pl.BlockSpec((1, PAIRS, 8, length), lambda b, m: (b, 0, 0, 0))],
        [shape((t, d)), shape((seqs, PAIRS, 8, length), F32)],
        [pltpu.VMEM((SEQ_LEN, length), F32)],
        (q, *keys, *values),
        "attend",
    )


def attend_back(q, keys, values, d_mixed, lse, meta, seqs, length):
    t, d = q.shape
    side = len(keys)
    ns = side * side
    kv = KV_HEADS * HEAD

    def body(meta, *refs):
        qr, kr, vr = refs[0], refs[1 : 1 + side], refs[1 + side : 1 + 2 * side]
        dm, lse = refs[1 + 2 * side : 3 + 2 * side]
        dq = refs[3 + 2 * side]
        dk = refs[4 + 2 * side : 4 + 3 * side]
        dv = refs[4 + 3 * side : 4 + 4 * side]
        bias = refs[-1]
        fill_bias(meta, bias, ns, length)

        def pair(p, _):
            wide = pl.ds(pl.multiple_of(p * 2 * GROUP * HEAD, 128), 2 * GROUP * HEAD)
            narrow = pl.ds(pl.multiple_of(p * 2 * HEAD, 128), 2 * HEAD)
            qp = qr[:, wide]
            dp = dm[:, wide]
            kp = key_rows(kr, narrow, side, True)
            vp = key_rows(vr, narrow, side, False)
            dqs, dks, dvs = [], [], []
            for g in range(2):
                k = kp[:, g * HEAD : (g + 1) * HEAD]
                v = vp[:, g * HEAD : (g + 1) * HEAD]
                kt = k.T
                d_key = d_value = None
                for h in range(GROUP):
                    i = g * GROUP + h
                    one = qp[:, i * HEAD : (i + 1) * HEAD] * jnp.asarray(SCALE, BF16)
                    up = dp[:, i * HEAD : (i + 1) * HEAD]
                    score = dot(k, one, 1, 1) + bias[...]
                    w = jnp.exp(score - lse[0, p, pl.ds(i, 1), :])
                    moved = w * dot(v, up, 1, 1)
                    ds = (moved - w * jnp.sum(moved, 0, keepdims=True)).astype(BF16)
                    dqs.append(dot(kt, ds) * SCALE)
                    a = dot(ds, one)
                    b = dot(w.astype(BF16), up)
                    d_key = a if d_key is None else d_key + a
                    d_value = b if d_value is None else d_value + b
                dks.append(d_key)
                dvs.append(d_value)
            dq[:, wide] = jnp.concatenate(dqs, 0).T
            d_key = jnp.concatenate(dks, 1).astype(BF16)
            d_value = jnp.concatenate(dvs, 1).astype(BF16)
            for i in range(side):
                for j in range(side):
                    rows = slice((i * side + j) * length, (i * side + j + 1) * length)
                    dk[i][j, :, narrow] = d_key[rows]
                    dv[j][i, :, narrow] = d_value[rows]
            return 0

        lax.fori_loop(0, PAIRS, pair, 0)

    kv_spec = pl.BlockSpec((side, length, kv), lambda b, m: (0, b, 0))
    row = pl.BlockSpec((length, d), lambda b, m: (b, 0))
    out = call(
        body,
        (seqs,),
        (meta,),
        [row] + [kv_spec] * (2 * side) + [row, pl.BlockSpec((1, PAIRS, 8, length), lambda b, m: (b, 0, 0, 0))],
        [row] + [kv_spec] * (2 * side),
        [shape((t, d), F32)] + [shape((side, t, kv))] * (2 * side),
        [pltpu.VMEM((SEQ_LEN, length), F32)],
        (q, *keys, *values, d_mixed, lse),
        "attend_back",
    )
    return out[0], out[1 : 1 + side], out[1 + side :]


def out_section(big, d):
    ns = big.shape[0]
    lanes = ceil_lanes(d // ns)
    return pl.BlockSpec((1, d, lanes), lambda s: (s, 0, big.shape[2] // lanes - 1))


def after_attention(mixed, tokens, gain, big, nz):
    t, d = mixed.shape
    ns = big.shape[0]
    ow = d // ns

    def body(mx, tok, gn, w, mid, nm, nt, mc, sq, acc):
        s = pl.program_id(0)

        @pl.when(s == 0)
        def _():
            a, b = split_lanes(mx[...], nz)
            mc[0] = a
            mc[1] = b

        y = dot(mx[...], w[0][:, :ow])
        for i in range(ns):

            @pl.when(s == i)
            def _():
                acc[:, i * ow : (i + 1) * ow] = y

        @pl.when(s == ns - 1)
        def _():
            branch = acc[...]
            m = tok[...].astype(F32) + branch
            mid[...] = m
            sq[...] = jnp.sum(branch * branch, 0, keepdims=True)
            r = lax.rsqrt(jnp.mean(m * m, -1, keepdims=True) + EPSILON)
            n = (m * r * gn[...]).astype(BF16)
            nm[...] = n
            a, b = split_rows(n.T, nz)
            nt[0] = a
            nt[1] = b

    return call(
        body,
        (ns,),
        (),
        [once((t, d)), once((t, d)), once((1, d)), out_section(big, d)],
        [whole((t, d)), whole((t, d)), whole((2, d // 2, t)), whole((2, t, d // 2)), whole((1, d))],
        [shape((t, d), F32), shape((t, d)), shape((2, d // 2, t)), shape((2, t, d // 2)), shape((1, d), F32)],
        [pltpu.VMEM((t, d), F32)],
        (mixed, tokens, gain, big),
        "after_attention",
    )


def feed_forward(normed, middle, cotangent, gain, big, nb, ff):
    t, d = normed.shape
    ns = big.shape[0]
    ratio, width, rows = nb // ns, ff // nb, d // nb
    section = ceil_lanes(ff // ns)
    lanes = width if ratio > 1 else section
    steps = nb

    def body(nm, mid, cot, gn, g_w, u_w, d_w, out, hid, dg, du, dmid, datt, datt_t, gg, sq, acc, dn):
        j = pl.program_id(0)
        n, c = nm[...], cot[...]
        gw_, uw_ = g_w[0][:, :width], u_w[0][:, :width]
        dw_ = jnp.concatenate(
            [d_w[s, :, i * width : (i + 1) * width] for s in range(ns) for i in range(ratio)], 0
        )
        g = dot(n, gw_)
        u = dot(n, uw_)
        dh = dot(c, dw_)
        sg = 1.0 / (1.0 + jnp.exp(-g))
        silu = g * sg
        h = (silu * u).astype(BF16)
        d_gate = (dh * u * sg * (1.0 + g * (1.0 - sg))).astype(BF16)
        d_up = (dh * silu).astype(BF16)
        hid[0, 0] = h
        dg[0] = d_gate
        du[0] = d_up
        a = dot(h, dw_, 1, 1)
        b = dot(d_gate, gw_, 1, 1) + dot(d_up, uw_, 1, 1)

        @pl.when(j == 0)
        def _():
            acc[...] = a
            dn[...] = b

        @pl.when(j > 0)
        def _():
            acc[...] += a
            dn[...] += b

        @pl.when(j == steps - 1)
        def _():
            m = mid[...]
            branch = acc[...]
            out[...] = (m + branch).astype(BF16)
            sq[...] = jnp.sum(branch * branch, 0, keepdims=True)
            r = lax.rsqrt(jnp.mean(m * m, -1, keepdims=True) + EPSILON)
            up_ = dn[...]
            gg[...] = jnp.sum(up_ * (m * r), 0, keepdims=True)
            scaled = up_ * gn[...]
            inner = jnp.sum(scaled * m, -1, keepdims=True)
            back = c.astype(F32) + r * scaled - m * (r * r * r * inner * (1.0 / d))
            dmid[...] = back
            low = back.astype(BF16)
            datt[...] = low
            datt_t[...] = low.T

    return call(
        body,
        (steps,),
        (),
        [once((t, d)), once((t, d)), once((t, d)), once((1, d)),
         pl.BlockSpec((1, d, lanes), lambda j: (j // ratio, 0, section // lanes + j % ratio)),
         pl.BlockSpec((1, d, lanes), lambda j: (j // ratio, 0, 2 * section // lanes + j % ratio)),
         pl.BlockSpec((ns, rows, section), lambda j: (0, j, 0))],
        [whole((t, d)),
         pl.BlockSpec((1, 1, t, width), lambda j: (j % 2, j // 2, 0, 0)),
         pl.BlockSpec((1, t, width), lambda j: (j // ratio, 0, j % ratio)),
         pl.BlockSpec((1, t, width), lambda j: (j // ratio, 0, j % ratio)),
         whole((t, d)), whole((t, d)), whole((d, t)), whole((1, d)), whole((1, d))],
        [shape((t, d)), shape((2, nb // 2, t, width)), shape((ns, t, ff // ns)), shape((ns, t, ff // ns)),
         shape((t, d), F32), shape((t, d)), shape((d, t)), shape((1, d), F32), shape((1, d), F32)],
        [pltpu.VMEM((t, d), F32), pltpu.VMEM((t, d), F32)],
        (normed, middle, cotangent, gain, big, big, big),
        "feed_forward",
    )


def mixed_back(d_attn, big):
    t, d = d_attn.shape
    ns = big.shape[0]
    ow = d // ns

    def body(da, w, out, acc):
        s = pl.program_id(0)
        weight = w[0][:, :ow]
        for i in range(ns):

            @pl.when(s == i)
            def _():
                y = dot(da[:, i * ow : (i + 1) * ow], weight, 1, 1)
                acc[...] = y if i == 0 else acc[...] + y

        @pl.when(s == ns - 1)
        def _():
            out[...] = acc[...].astype(BF16)

    return call(
        body,
        (ns,),
        (),
        [once((t, d)), out_section(big, d)],
        whole((t, d)),
        shape((t, d)),
        [pltpu.VMEM((t, d), F32)],
        (d_attn, big),
        "mixed_back",
    )


def qkv_back(dq, dk, dv, cosine, sine, tokens, d_middle, gain, att):
    t, d = tokens.shape
    ns, _, wide = att.shape
    qw, kw = d // ns, KV_HEADS * HEAD // ns
    used = qw + 2 * kw
    pad = -(-used // 128) * 128
    kv = KV_HEADS * HEAD

    def body(dq, dk, dv, cs, sn, tok, dmid, gn, w, blk, out, gg, q_s, k_s, v_s, acc):
        s = pl.program_id(0)

        @pl.when(s == 0)
        def _():
            q_s[...] = turn(dq[...], cs[...], -sn[...]).astype(BF16)
            k_s[...] = turn(dk[...], cs[...], -sn[...]).astype(BF16)
            v_s[...] = dv[...].astype(BF16)

        weight = w[0][:, :used]
        for i in range(ns):

            @pl.when(s == i)
            def _():
                parts = [q_s[:, i * qw : (i + 1) * qw], k_s[:, i * kw : (i + 1) * kw], v_s[:, i * kw : (i + 1) * kw]]
                b = jnp.concatenate(parts, 1)
                blk[0] = jnp.concatenate([b, jnp.zeros((t, pad - used), BF16)], 1) if pad > used else b
                y = dot(b, weight, 1, 1)
                acc[...] = y if i == 0 else acc[...] + y

        @pl.when(s == ns - 1)
        def _():
            x = tok[...].astype(F32)
            r = lax.rsqrt(jnp.mean(x * x, -1, keepdims=True) + EPSILON)
            up_ = acc[...]
            gg[...] = jnp.sum(up_ * (x * r), 0, keepdims=True)
            scaled = up_ * gn[...]
            inner = jnp.sum(scaled * x, -1, keepdims=True)
            out[...] = dmid[...] + r * scaled - x * (r * r * r * inner * (1.0 / d))

    return call(
        body,
        (ns,),
        (),
        [once((t, d)), once((t, kv)), once((t, kv)), once(cosine.shape), once(sine.shape),
         once((t, d)), once((t, d)), once((1, d)), pl.BlockSpec((1, d, wide), lambda s: (s, 0, 0))],
        [pl.BlockSpec((1, t, pad), lambda s: (s, 0, 0)), whole((t, d)), whole((1, d))],
        [shape((ns, t, pad)), shape((t, d), F32), shape((1, d), F32)],
        [pltpu.VMEM((t, d), BF16), pltpu.VMEM((t, kv), BF16), pltpu.VMEM((t, kv), BF16), pltpu.VMEM((t, d), F32)],
        (dq, dk, dv, cosine, sine, tokens, d_middle, gain, att),
        "qkv_back",
    )


def row_grads(picks, core, n_t, n_t2, blk, blk2):
    _, r, t = n_t.shape
    w = blk.shape[2]
    m = picks.shape[0]

    def body(pk, co, a, a2, g, g2, out):
        out[0] = (dot(a[0], g[0]) + dot(a2[...], g2[0])).astype(BF16)

    col = pl.BlockSpec((1, t, w), lambda i, pk, co: (pk[i], 0, 0))
    return call(
        body,
        (m,),
        (picks, core),
        [pl.BlockSpec((1, r, t), lambda i, pk, co: (co[0], 0, 0)), whole((r, t)), col, col],
        pl.BlockSpec((1, r, w), lambda i, pk, co: (i, 0, 0)),
        shape((m, r, w)),
        [],
        (n_t, n_t2, blk, blk2),
        "row_grads",
    )


def down_out_grads(picks, core, cot_t, cot_t2, hid, hid2, da_t, da_t2, mix, mix2, ns):
    d, t = cot_t.shape
    w = d // ns
    nz, hw, mw = hid.shape[1], hid.shape[3], mix.shape[2]
    m = picks.shape[0]

    def body(pk, co, c, c2, h, h2, a, a2, x, x2, out):
        for z in range(nz):
            out[0, :, z * hw : (z + 1) * hw] = (dot(c[...], h[0, z]) + dot(c2[...], h2[z])).astype(BF16)
        out[0, :, nz * hw :] = (dot(a[...], x[0]) + dot(a2[...], x2[...])).astype(BF16)

    row = pl.BlockSpec((w, t), lambda i, pk, co: (pk[i], 0))
    return call(
        body,
        (m,),
        (picks, core),
        [row, row, pl.BlockSpec((1, nz, t, hw), lambda i, pk, co: (co[0], 0, 0, 0)), whole((nz, t, hw)),
         row, row, pl.BlockSpec((1, t, mw), lambda i, pk, co: (co[0], 0, 0)), whole((t, mw))],
        pl.BlockSpec((1, w, nz * hw + mw), lambda i, pk, co: (i, 0, 0)),
        shape((m, w, nz * hw + mw)),
        [],
        (cot_t, cot_t2, hid, hid2, da_t, da_t2, mix, mix2),
        "down_out_grads",
    )


def solution(mesh):
    nb, ns = mesh.shape["batch"], mesh.shape["seq"]
    nz, side = nb // 2, math.isqrt(ns)
    sizes = {"z": nz, "c": 2, "y": side, "x": side}

    def pairs(axis, k):
        out = []
        if axis in "zc":
            for z in range(nz):
                for c in range(2):
                    to = ((z + k) % nz) * 2 + c if axis == "z" else z * 2 + (c + k) % 2
                    out.append((z * 2 + c, to))
            return "batch", out
        for y in range(side):
            for x in range(side):
                to = ((y + k) % side) * side + x if axis == "y" else y * side + (x + k) % side
                out.append((y * side + x, to))
        return "seq", out

    def push(value, axis, k):
        name, perm = pairs(axis, k)
        return lax.ppermute(value, name, perm)

    def fetch(value, axis, k):
        return push(value, axis, sizes[axis] - k)

    def fetch_plane(value, k, j):
        perm = [
            ((y + k) % side * side + (x + j) % side, y * side + x) for y in range(side) for x in range(side)
        ]
        return lax.ppermute(value, "seq", perm)

    def spread(value, first, second):
        near = jnp.stack([value] + [fetch(value, first, k) for k in range(1, side)])
        return [near] + [fetch(near, second, k) for k in range(1, side)]

    def add(parts):
        return functools.reduce(lambda a, b: a + b, [p.astype(F32) for p in parts])

    def reduce_plane(parts, first, second):
        got = [push(parts[k], first, k) for k in range(1, side)]
        mine = [parts[0]] + got
        sent = [push(add([m[j] for m in mine]).astype(BF16), second, j) for j in range(1, side)]
        return add([m[0] for m in mine] + sent)

    def reduce_z(slots, z):
        got = [push(slots((z + k) % nz).astype(BF16), "z", k) for k in range(1, nz)]
        return add([slots(z)] + got)

    def on_device(tokens, prefix, gain_a, w_q, w_k, w_v, w_o, gain_m, w_gate, w_up, w_down, cot):
        seqs, length, d = tokens.shape
        t = seqs * length
        tokens, cot = tokens.reshape(t, d), cot.reshape(t, d)
        gain_a, gain_m = gain_a[None], gain_m[None]
        bi, si = lax.axis_index("batch"), lax.axis_index("seq")
        z, c, y, x = bi // 2, bi % 2, si // side, si % side
        core = c.astype(jnp.int32)[None]

        def place(k, j):
            return ((y + k) % side) * side + (x + j) % side

        rows, qw, kw = d // nb, d // ns, KV_HEADS * HEAD // ns
        gw = w_gate.shape[1]
        dw = w_down.shape[0]
        ff = gw * ns
        widen = lambda v, lanes: jnp.pad(v, ((0, 0), (0, lanes - v.shape[1])))
        section = ceil_lanes(gw)
        down = w_down.T.reshape(nb // ns, rows, dw)
        down = jnp.concatenate(list(down), 1)
        big = jnp.concatenate(
            [widen(down, section), widen(w_gate, section), widen(w_up, section), widen(w_o, ceil_lanes(qw))], 1
        )
        big = lax.all_gather(big, ("seq", "batch"), axis=0, tiled=True).reshape(ns, d, -1)

        qkv = widen(jnp.concatenate([w_q, w_k, w_v], 1), ceil_lanes(qw + 2 * kw))
        column = jnp.stack([qkv] + [fetch(qkv, "z", k) for k in range(1, nz)])
        plane = [column if k + j == 0 else fetch_plane(column, k, j) for k in range(side) for j in range(side)]
        blocks = plane + [push(v, "c", 1) for v in plane]
        where = [place(k, j) for k in range(side) for j in range(side)]
        where += [((z + k) % nz) * 2 + (c + i) % 2 for i in range(2) for k in range(nz)]
        where = jnp.stack(where).astype(jnp.int32)

        position = si * length + jnp.arange(length, dtype=jnp.int32)
        half = HEAD // 2
        frequency = 10000.0 ** (-(jnp.arange(half, dtype=F32) * 2.0) / (2.0 * half))
        angles = position.astype(F32)[:, None] * frequency[None, :]
        cosine = jnp.tile(jnp.cos(angles), (seqs, 4))
        sine = jnp.sin(angles)
        sine = jnp.tile(jnp.concatenate([-sine, sine], 1), (seqs, 2))
        held = jnp.stack([place(k, j) for k in range(side) for j in range(side)])
        meta = jnp.concatenate([(si * length)[None], held * length, prefix]).astype(jnp.int32)

        cot_t = cot.T
        cot_t2 = push(cot_t, "c", 1)

        w_qkv, na_t, q, k, v = project(tokens, gain_a, cosine, sine, blocks, where, nz)
        w_qkv = w_qkv.reshape(ns, d, -1)
        keys = spread(k, "x", "y")
        values = spread(v, "y", "x")
        mixed, lse = attend(q, keys, values, meta, seqs, length)
        middle, normed_m, nm_t, mix, sq_a = after_attention(mixed, tokens, gain_m, big, nz)
        layer_out, hid, d_gate, d_up, d_middle, d_attn, da_t, gain_m_part, sq_m = feed_forward(
            normed_m, middle, cot, gain_m, big, nb, ff
        )
        other = lambda v: push(lax.dynamic_index_in_dim(v, 1 - c, 0, False), "c", 1)
        na_t2, nm_t2, mix2, hid2 = other(na_t), other(nm_t), other(mix), other(hid)
        d_gate2, d_up2, da_t2 = push(d_gate, "c", 1), push(d_up, "c", 1), push(da_t, "c", 1)
        d_mixed = mixed_back(d_attn, big)

        y_first = [jnp.stack([place(k, j) for j in range(side)]).astype(jnp.int32) for k in range(side)]
        x_first = [jnp.stack([place(j, k) for j in range(side)]).astype(jnp.int32) for k in range(side)]
        order = list(range(1, side)) + [0]
        g_gate, g_up, g_do = [None] * side, [None] * side, [None] * side
        for i in order:
            g_gate[i] = row_grads(y_first[i], core, nm_t, nm_t2, d_gate, d_gate2)
            g_up[i] = row_grads(x_first[i], core, nm_t, nm_t2, d_up, d_up2)
            g_do[i] = down_out_grads(x_first[i], core, cot_t, cot_t2, hid, hid2, da_t, da_t2, mix, mix2, ns)

        def by_rows(v):
            v = v.astype(BF16).reshape(nz, rows, -1)
            return reduce_z(lambda i: lax.dynamic_index_in_dim(v, i, 0, False), z)

        g_gate = by_rows(reduce_plane(g_gate, "y", "x"))
        g_up = by_rows(reduce_plane(g_up, "x", "y"))
        do = reduce_plane(g_do, "x", "y").astype(BF16)
        split = nz * dw
        do_d = do[:, :split].reshape(qw, nz, -1)
        do_o = do[:, split:].reshape(qw, nz, -1)
        at = lambda v, i: lax.dynamic_index_in_dim(v, i, 1, False)
        do = reduce_z(lambda i: jnp.concatenate([at(do_d, i), at(do_o, i)], 1), z)

        dq, dk, dv = attend_back(q, keys, values, d_mixed, lse, meta, seqs, length)
        dk = reduce_plane(dk, "y", "x")
        dv = reduce_plane(dv, "x", "y")
        blk, input_grad, gain_a_part = qkv_back(
            dq, dk, dv, cosine, sine, tokens, d_middle, gain_a, w_qkv
        )
        blk2 = push(blk, "c", 1)
        g_qkv = [None] * side
        for i in order:
            g_qkv[i] = row_grads(y_first[i], core, na_t, na_t2, blk, blk2)
        g_qkv = by_rows(reduce_plane(g_qkv, "y", "x"))

        inputs = tokens.astype(F32)
        sums = jnp.concatenate([gain_a_part, gain_m_part, sq_a, sq_m, jnp.sum(inputs * inputs, 0, keepdims=True)], 0)
        for axis in "cyxz":
            sums = add([sums] + [push(sums, axis, k) for k in range(1, sizes[axis])])
        entries = t * d * nb * ns
        rms = jnp.sqrt(jnp.sum(sums[jnp.array([4, 2, 3])], 1) / entries)
        return (
            layer_out.reshape(seqs, length, d),
            input_grad.reshape(seqs, length, d),
            sums[0],
            g_qkv[:, :qw],
            g_qkv[:, qw : qw + kw],
            g_qkv[:, qw + kw : qw + 2 * kw],
            do[:, dw:].T,
            sums[1],
            g_gate,
            g_up,
            do[:, :dw].T,
            rms,
        )

    rows, flat, copied = P("batch", "seq", None), P("batch", "seq"), P()
    return jax.shard_map(
        on_device,
        mesh=mesh,
        in_specs=(rows, P("batch"), copied, flat, flat, flat, flat, copied, flat, flat, flat, rows),
        out_specs=(rows, rows, copied, flat, flat, flat, flat, copied, flat, flat, flat, copied),
        check_vma=False,
    )
```

```python
import functools
import math

import jax
import jax.numpy as jnp
from jax import lax
from jax.experimental import pallas as pl
from jax.experimental.pallas import tpu as pltpu
from jax.sharding import PartitionSpec as P

HEADS = 18
KV_HEADS = 6
HEAD = 64
SEQ_LEN = 1024
GROUP = HEADS // KV_HEADS
PAIRS = KV_HEADS // 2
EPSILON = 1e-05
MASKED = -1e30
SCALE = HEAD ** (-0.5)
F32 = jnp.float32
BF16 = jnp.bfloat16


def dot(a, b, ca=1, cb=0):
    return lax.dot_general(a, b, (((ca,), (cb,)), ((), ())), preferred_element_type=F32)


def whole(shape, **kw):
    zeros = (0,) * len(shape)
    return pl.BlockSpec(shape, lambda *_: zeros, **kw)


def once(shape):
    return whole(shape, pipeline_mode=pl.Buffered(1))


def call(body, grid, scalars, in_specs, out_specs, out_shape, scratch, args):
    return pl.pallas_call(
        body,
        grid_spec=pltpu.PrefetchScalarGridSpec(
            num_scalar_prefetch=len(scalars),
            grid=grid,
            in_specs=in_specs,
            out_specs=out_specs,
            scratch_shapes=scratch,
        ),
        out_shape=out_shape,
        compiler_params=pltpu.CompilerParams(
            dimension_semantics=("arbitrary",) * len(grid), vmem_limit_bytes=60 * 2**20
        ),
    )(*scalars, *args)


def shape(dims, kind=BF16):
    return jax.ShapeDtypeStruct(dims, kind)


def swap_halves(v):
    lane = lax.broadcasted_iota(jnp.int32, v.shape, 1) % HEAD
    n = v.shape[1]
    return jnp.where(lane < HEAD // 2, pltpu.roll(v, n - HEAD // 2, 1), pltpu.roll(v, HEAD // 2, 1))


def turn(v, cosine, sine):
    width = cosine.shape[1]
    parts = []
    for j in range(v.shape[1] // width):
        u = v[:, j * width : (j + 1) * width]
        parts.append(u * cosine + swap_halves(u) * sine)
    return jnp.concatenate(parts, 1)


def split_rows(value, nz):
    rows = value.shape[0] // (2 * nz)
    take = lambda c: jnp.concatenate(
        [value[(2 * z + c) * rows : (2 * z + c + 1) * rows] for z in range(nz)], 0
    )
    return take(0), take(1)


def split_lanes(value, nz):
    cols = value.shape[1] // (2 * nz)
    take = lambda c: jnp.concatenate(
        [value[:, (2 * z + c) * cols : (2 * z + c + 1) * cols] for z in range(nz)], 1
    )
    return take(0), take(1)


def ceil_lanes(n):
    return -(-n // 128) * 128


def project(tokens, gain, cosine, sine, blocks, where, nz):
    t, d = tokens.shape
    _, rows, wide = blocks[0].shape
    ns, nb = len(blocks) // 2, 2 * nz
    kv = KV_HEADS * HEAD
    qw, kw = d // ns, kv // ns

    def body(at, tok, gn, cs, sn, *refs):
        parts, (w, nt, q, k, v, q_s, k_s, v_s) = refs[: 2 * ns], refs[2 * ns :]
        for p in range(ns):
            for c in range(2):
                for z in range(nz):
                    w[at[p], at[ns + c * nz + z]] = parts[c * ns + p][z]
        x = tok[...].astype(F32)
        r = lax.rsqrt(jnp.mean(x * x, -1, keepdims=True) + EPSILON)
        n = (x * r * gn[...]).astype(BF16)
        a, b = split_rows(n.T, nz)
        nt[0] = a
        nt[1] = b
        for i in range(ns):
            weight = jnp.concatenate([w[i, j] for j in range(nb)], 0)
            y = dot(n, weight)
            q_s[:, i * qw : (i + 1) * qw] = y[:, :qw]
            k_s[:, i * kw : (i + 1) * kw] = y[:, qw : qw + kw]
            v_s[:, i * kw : (i + 1) * kw] = y[:, qw + kw : qw + 2 * kw]
        q[...] = turn(q_s[...], cs[...], sn[...]).astype(BF16)
        k[...] = turn(k_s[...], cs[...], sn[...]).astype(BF16)
        v[...] = v_s[...].astype(BF16)

    return call(
        body,
        (1,),
        (where,),
        [once((t, d)), once((1, d)), once(cosine.shape), once(sine.shape)] + [once(v.shape) for v in blocks],
        [whole((ns, nb, rows, wide)), whole((2, d // 2, t)), whole((t, d)), whole((t, kv)), whole((t, kv))],
        [shape((ns, nb, rows, wide)), shape((2, d // 2, t)), shape((t, d)), shape((t, kv)), shape((t, kv))],
        [pltpu.VMEM((t, d), F32), pltpu.VMEM((t, kv), F32), pltpu.VMEM((t, kv), F32)],
        (tokens, gain, cosine, sine, *blocks),
    )


def fill_bias(meta, bias, ns, length, b):
    prefix = meta[1 + ns + b]
    for i in range(ns):
        key = meta[1 + i] + lax.broadcasted_iota(jnp.int32, (length, length), 0)
        row = meta[0] + lax.broadcasted_iota(jnp.int32, (length, length), 1)
        bias[i * length : (i + 1) * length, :] = jnp.where(
            (key <= row) | (key < prefix), 0.0, MASKED
        ).astype(F32)


def key_rows(refs, lanes, side, first_major):
    parts = []
    for i in range(side):
        for j in range(side):
            ref = refs[i] if first_major else refs[j]
            parts.append(ref[j if first_major else i, :, lanes])
    return jnp.concatenate(parts, 0)


def attend(q, keys, values, meta, seqs, length):
    t, d = q.shape
    side = len(keys)
    ns = side * side
    kv = KV_HEADS * HEAD

    def body(meta, *refs):
        qr, kr, vr = refs[0], refs[1 : 1 + side], refs[1 + side : 1 + 2 * side]
        out, lse, bias = refs[1 + 2 * side :]
        fill_bias(meta, bias, ns, length, pl.program_id(0))

        def pair(p, _):
            wide = pl.ds(pl.multiple_of(p * 2 * GROUP * HEAD, 128), 2 * GROUP * HEAD)
            narrow = pl.ds(pl.multiple_of(p * 2 * HEAD, 128), 2 * HEAD)
            qp = qr[:, wide]
            kp = key_rows(kr, narrow, side, True)
            vp = key_rows(vr, narrow, side, False)
            outs = []
            for g in range(2):
                k = kp[:, g * HEAD : (g + 1) * HEAD]
                vt = vp[:, g * HEAD : (g + 1) * HEAD].T
                for h in range(GROUP):
                    i = g * GROUP + h
                    one = qp[:, i * HEAD : (i + 1) * HEAD] * jnp.asarray(SCALE, BF16)
                    score = dot(k, one, 1, 1) + bias[...]
                    top = jnp.max(score, 0, keepdims=True)
                    e = jnp.exp(score - top)
                    total = jnp.sum(e, 0, keepdims=True)
                    outs.append(dot(vt, e.astype(BF16)) * (1.0 / total))
                    lse[0, p, pl.ds(i, 1), :] = top + jnp.log(total)
            out[:, wide] = jnp.concatenate(outs, 0).T.astype(BF16)
            return 0

        lax.fori_loop(0, PAIRS, pair, 0)

    kv_spec = pl.BlockSpec((side, length, kv), lambda b, m: (0, b, 0))
    row = pl.BlockSpec((length, d), lambda b, m: (b, 0))
    return call(
        body,
        (seqs,),
        (meta,),
        [row] + [kv_spec] * (2 * side),
        [row, pl.BlockSpec((1, PAIRS, 8, length), lambda b, m: (b, 0, 0, 0))],
        [shape((t, d)), shape((seqs, PAIRS, 8, length), F32)],
        [pltpu.VMEM((SEQ_LEN, length), F32)],
        (q, *keys, *values),
    )


def attend_back(q, keys, values, d_mixed, lse, meta, seq, length):
    _, d = q.shape
    side = len(keys)
    ns = side * side
    kv = KV_HEADS * HEAD

    def body(meta, *refs):
        qr, kr, vr = refs[0], refs[1 : 1 + side], refs[1 + side : 1 + 2 * side]
        dm, lse = refs[1 + 2 * side : 3 + 2 * side]
        dq = refs[3 + 2 * side]
        dk = refs[4 + 2 * side : 4 + 3 * side]
        dv = refs[4 + 3 * side : 4 + 4 * side]
        bias = refs[-1]
        fill_bias(meta, bias, ns, length, seq)

        def pair(p, _):
            wide = pl.ds(pl.multiple_of(p * 2 * GROUP * HEAD, 128), 2 * GROUP * HEAD)
            narrow = pl.ds(pl.multiple_of(p * 2 * HEAD, 128), 2 * HEAD)
            qp = qr[:, wide]
            dp = dm[:, wide]
            kp = key_rows(kr, narrow, side, True)
            vp = key_rows(vr, narrow, side, False)
            dqs, dks, dvs = [], [], []
            for g in range(2):
                k = kp[:, g * HEAD : (g + 1) * HEAD]
                v = vp[:, g * HEAD : (g + 1) * HEAD]
                kt = k.T
                d_key = d_value = None
                for h in range(GROUP):
                    i = g * GROUP + h
                    one = qp[:, i * HEAD : (i + 1) * HEAD] * jnp.asarray(SCALE, BF16)
                    up = dp[:, i * HEAD : (i + 1) * HEAD]
                    score = dot(k, one, 1, 1) + bias[...]
                    w = jnp.exp(score - lse[0, p, pl.ds(i, 1), :])
                    moved = w * dot(v, up, 1, 1)
                    ds = (moved - w * jnp.sum(moved, 0, keepdims=True)).astype(BF16)
                    dqs.append(dot(kt, ds) * SCALE)
                    a = dot(ds, one)
                    b = dot(w.astype(BF16), up)
                    d_key = a if d_key is None else d_key + a
                    d_value = b if d_value is None else d_value + b
                dks.append(d_key)
                dvs.append(d_value)
            dq[:, wide] = jnp.concatenate(dqs, 0).T
            d_key = jnp.concatenate(dks, 1).astype(BF16)
            d_value = jnp.concatenate(dvs, 1).astype(BF16)
            for i in range(side):
                for j in range(side):
                    rows = slice((i * side + j) * length, (i * side + j + 1) * length)
                    dk[i][j, :, narrow] = d_key[rows]
                    dv[j][i, :, narrow] = d_value[rows]
            return 0

        lax.fori_loop(0, PAIRS, pair, 0)

    kv_spec = pl.BlockSpec((side, length, kv), lambda b, m: (0, seq, 0))
    row = pl.BlockSpec((length, d), lambda b, m: (seq, 0))
    out = call(
        body,
        (1,),
        (meta,),
        [row] + [kv_spec] * (2 * side) + [row, pl.BlockSpec((1, PAIRS, 8, length), lambda b, m: (seq, 0, 0, 0))],
        [whole((length, d))] + [whole((side, length, kv))] * (2 * side),
        [shape((length, d), F32)] + [shape((side, length, kv))] * (2 * side),
        [pltpu.VMEM((SEQ_LEN, length), F32)],
        (q, *keys, *values, d_mixed, lse),
    )
    return out[0], out[1 : 1 + side], out[1 + side :]


def out_section(big, d):
    ns = big.shape[0]
    lanes = ceil_lanes(d // ns)
    return pl.BlockSpec((1, d, lanes), lambda s: (s, 0, big.shape[2] // lanes - 1))


def after_attention(mixed, tokens, gain, big, nz):
    t, d = mixed.shape
    ns = big.shape[0]
    ow = d // ns

    def body(mx, tok, gn, w, mid, nm, nt, mc, sq, acc):
        s = pl.program_id(0)

        @pl.when(s == 0)
        def _():
            a, b = split_lanes(mx[...], nz)
            mc[0] = a
            mc[1] = b

        y = dot(mx[...], w[0][:, :ow])
        for i in range(ns):

            @pl.when(s == i)
            def _():
                acc[:, i * ow : (i + 1) * ow] = y

        @pl.when(s == ns - 1)
        def _():
            branch = acc[...]
            m = tok[...].astype(F32) + branch
            mid[...] = m
            sq[...] = jnp.sum(branch * branch, 0, keepdims=True)
            r = lax.rsqrt(jnp.mean(m * m, -1, keepdims=True) + EPSILON)
            n = (m * r * gn[...]).astype(BF16)
            nm[...] = n
            a, b = split_rows(n.T, nz)
            nt[0] = a
            nt[1] = b

    return call(
        body,
        (ns,),
        (),
        [once((t, d)), once((t, d)), once((1, d)), out_section(big, d)],
        [whole((t, d)), whole((t, d)), whole((2, d // 2, t)), whole((2, t, d // 2)), whole((1, d))],
        [shape((t, d), F32), shape((t, d)), shape((2, d // 2, t)), shape((2, t, d // 2)), shape((1, d), F32)],
        [pltpu.VMEM((t, d), F32)],
        (mixed, tokens, gain, big),
    )


def feed_forward(normed, middle, cotangent, gain, big, nb, ff):
    t, d = normed.shape
    ns = big.shape[0]
    ratio, width, rows = nb // ns, ff // nb, d // nb
    section = ceil_lanes(ff // ns)
    lanes = width if ratio > 1 else section
    steps = nb

    def body(nm, mid, cot, gn, g_w, u_w, d_w, out, hid, dg, du, dmid, datt, datt_t, gg, sq, acc, dn):
        j = pl.program_id(0)
        n, c = nm[...], cot[...]
        gw_, uw_ = g_w[0][:, :width], u_w[0][:, :width]
        dw_ = jnp.concatenate(
            [d_w[s, :, i * width : (i + 1) * width] for s in range(ns) for i in range(ratio)], 0
        )
        g = dot(n, gw_)
        u = dot(n, uw_)
        dh = dot(c, dw_)
        sg = 1.0 / (1.0 + jnp.exp(-g))
        silu = g * sg
        h = (silu * u).astype(BF16)
        d_gate = (dh * u * sg * (1.0 + g * (1.0 - sg))).astype(BF16)
        d_up = (dh * silu).astype(BF16)
        hid[0, 0] = h
        dg[0] = d_gate
        du[0] = d_up
        a = dot(h, dw_, 1, 1)
        b = dot(d_gate, gw_, 1, 1) + dot(d_up, uw_, 1, 1)

        @pl.when(j == 0)
        def _():
            acc[...] = a
            dn[...] = b

        @pl.when(j > 0)
        def _():
            acc[...] += a
            dn[...] += b

        @pl.when(j == steps - 1)
        def _():
            m = mid[...]
            branch = acc[...]
            out[...] = (m + branch).astype(BF16)
            sq[...] = jnp.sum(branch * branch, 0, keepdims=True)
            r = lax.rsqrt(jnp.mean(m * m, -1, keepdims=True) + EPSILON)
            up_ = dn[...]
            gg[...] = jnp.sum(up_ * (m * r), 0, keepdims=True)
            scaled = up_ * gn[...]
            inner = jnp.sum(scaled * m, -1, keepdims=True)
            back = c.astype(F32) + r * scaled - m * (r * r * r * inner * (1.0 / d))
            dmid[...] = back
            low = back.astype(BF16)
            datt[...] = low
            datt_t[...] = low.T

    return call(
        body,
        (steps,),
        (),
        [once((t, d)), once((t, d)), once((t, d)), once((1, d)),
         pl.BlockSpec((1, d, lanes), lambda j: (j // ratio, 0, section // lanes + j % ratio)),
         pl.BlockSpec((1, d, lanes), lambda j: (j // ratio, 0, 2 * section // lanes + j % ratio)),
         pl.BlockSpec((ns, rows, section), lambda j: (0, j, 0))],
        [whole((t, d)),
         pl.BlockSpec((1, 1, t, width), lambda j: (j % 2, j // 2, 0, 0)),
         pl.BlockSpec((1, t, width), lambda j: (j // ratio, 0, j % ratio)),
         pl.BlockSpec((1, t, width), lambda j: (j // ratio, 0, j % ratio)),
         whole((t, d)), whole((t, d)), whole((d, t)), whole((1, d)), whole((1, d))],
        [shape((t, d)), shape((2, nb // 2, t, width)), shape((ns, t, ff // ns)), shape((ns, t, ff // ns)),
         shape((t, d), F32), shape((t, d)), shape((d, t)), shape((1, d), F32), shape((1, d), F32)],
        [pltpu.VMEM((t, d), F32), pltpu.VMEM((t, d), F32)],
        (normed, middle, cotangent, gain, big, big, big),
    )


def mixed_back(d_attn, big):
    t, d = d_attn.shape
    ns = big.shape[0]
    ow = d // ns

    def body(da, w, out, acc):
        s = pl.program_id(0)
        weight = w[0][:, :ow]
        for i in range(ns):

            @pl.when(s == i)
            def _():
                y = dot(da[:, i * ow : (i + 1) * ow], weight, 1, 1)
                acc[...] = y if i == 0 else acc[...] + y

        @pl.when(s == ns - 1)
        def _():
            out[...] = acc[...].astype(BF16)

    return call(
        body,
        (ns,),
        (),
        [once((t, d)), out_section(big, d)],
        whole((t, d)),
        shape((t, d)),
        [pltpu.VMEM((t, d), F32)],
        (d_attn, big),
    )


def query_back(dqs, cosine, sine, w_qkv):
    length, d = dqs[0].shape
    n = len(dqs)
    t = n * length
    ns, _, _ = w_qkv.shape
    qw = d // ns
    pad = ceil_lanes(qw)

    def body(*refs):
        cs, sn, w, blk, acc, q_s = refs[n:]
        s = pl.program_id(0)

        @pl.when(s == 0)
        def _():
            for i in range(n):
                rows = slice(i * length, (i + 1) * length)
                q_s[rows, :] = turn(refs[i][...], cs[rows, :], -sn[rows, :]).astype(BF16)

        weight = w[0][:, :qw]
        for i in range(ns):

            @pl.when(s == i)
            def _():
                b = q_s[:, i * qw : (i + 1) * qw]
                blk[0] = jnp.concatenate([b, jnp.zeros((t, pad - qw), BF16)], 1) if pad > qw else b
                y = dot(b, weight, 1, 1)
                acc[...] = y if i == 0 else acc[...] + y

    return call(
        body,
        (ns,),
        (),
        [once((length, d))] * n + [once(cosine.shape), once(sine.shape), pl.BlockSpec((1, d, pad), lambda s: (s, 0, 0))],
        [pl.BlockSpec((1, t, pad), lambda s: (s, 0, 0)), whole((t, d))],
        [shape((ns, t, pad)), shape((t, d), F32)],
        [pltpu.VMEM((t, d), BF16)],
        (*dqs, cosine, sine, w_qkv),
    )


def key_value_back(dk, dv, from_q, cosine, sine, tokens, d_middle, gain, w_qkv):
    t, d = tokens.shape
    ns, _, wide = w_qkv.shape
    qw, kw = d // ns, KV_HEADS * HEAD // ns
    pad = ceil_lanes(2 * kw)
    kv = KV_HEADS * HEAD

    def body(dk, dv, fq, cs, sn, tok, dmid, gn, w, blk, out, gg, k_s, v_s, acc):
        s = pl.program_id(0)

        @pl.when(s == 0)
        def _():
            k_s[...] = turn(dk[...], cs[...], -sn[...]).astype(BF16)
            v_s[...] = dv[...].astype(BF16)

        weight = w[0][:, qw : qw + 2 * kw]
        for i in range(ns):

            @pl.when(s == i)
            def _():
                b = jnp.concatenate([k_s[:, i * kw : (i + 1) * kw], v_s[:, i * kw : (i + 1) * kw]], 1)
                blk[0] = jnp.concatenate([b, jnp.zeros((t, pad - 2 * kw), BF16)], 1) if pad > 2 * kw else b
                acc[...] = (fq[...] if i == 0 else acc[...]) + dot(b, weight, 1, 1)

        @pl.when(s == ns - 1)
        def _():
            x = tok[...].astype(F32)
            r = lax.rsqrt(jnp.mean(x * x, -1, keepdims=True) + EPSILON)
            up_ = acc[...]
            gg[...] = jnp.sum(up_ * (x * r), 0, keepdims=True)
            scaled = up_ * gn[...]
            inner = jnp.sum(scaled * x, -1, keepdims=True)
            out[...] = dmid[...] + r * scaled - x * (r * r * r * inner * (1.0 / d))

    return call(
        body,
        (ns,),
        (),
        [once((t, kv)), once((t, kv)), once((t, d)), once(cosine.shape), once(sine.shape),
         once((t, d)), once((t, d)), once((1, d)), pl.BlockSpec((1, d, wide), lambda s: (s, 0, 0))],
        [pl.BlockSpec((1, t, pad), lambda s: (s, 0, 0)), whole((t, d)), whole((1, d))],
        [shape((ns, t, pad)), shape((t, d), F32), shape((1, d), F32)],
        [pltpu.VMEM((t, kv), BF16), pltpu.VMEM((t, kv), BF16), pltpu.VMEM((t, d), F32)],
        (dk, dv, from_q, cosine, sine, tokens, d_middle, gain, w_qkv),
    )


def row_grads(picks, core, n_t, n_t2, blk, blk2):
    _, r, t = n_t.shape
    w = blk.shape[2]
    m = picks.shape[0]

    def body(pk, co, a, a2, g, g2, out):
        out[0] = (dot(a[0], g[0]) + dot(a2[...], g2[0])).astype(BF16)

    col = pl.BlockSpec((1, t, w), lambda i, pk, co: (pk[i], 0, 0))
    return call(
        body,
        (m,),
        (picks, core),
        [pl.BlockSpec((1, r, t), lambda i, pk, co: (co[0], 0, 0)), whole((r, t)), col, col],
        pl.BlockSpec((1, r, w), lambda i, pk, co: (i, 0, 0)),
        shape((m, r, w)),
        [],
        (n_t, n_t2, blk, blk2),
    )


def down_out_grads(picks, core, cot_t, cot_t2, hid, hid2, da_t, da_t2, mix, mix2, ns):
    d, t = cot_t.shape
    w = d // ns
    nz, hw, mw = hid.shape[1], hid.shape[3], mix.shape[2]
    m = picks.shape[0]

    def body(pk, co, c, c2, h, h2, a, a2, x, x2, out):
        for z in range(nz):
            out[0, :, z * hw : (z + 1) * hw] = (dot(c[...], h[0, z]) + dot(c2[...], h2[z])).astype(BF16)
        out[0, :, nz * hw :] = (dot(a[...], x[0]) + dot(a2[...], x2[...])).astype(BF16)

    row = pl.BlockSpec((w, t), lambda i, pk, co: (pk[i], 0))
    return call(
        body,
        (m,),
        (picks, core),
        [row, row, pl.BlockSpec((1, nz, t, hw), lambda i, pk, co: (co[0], 0, 0, 0)), whole((nz, t, hw)),
         row, row, pl.BlockSpec((1, t, mw), lambda i, pk, co: (co[0], 0, 0)), whole((t, mw))],
        pl.BlockSpec((1, w, nz * hw + mw), lambda i, pk, co: (i, 0, 0)),
        shape((m, w, nz * hw + mw)),
        [],
        (cot_t, cot_t2, hid, hid2, da_t, da_t2, mix, mix2),
    )


def solution(mesh):
    nb, ns = mesh.shape["batch"], mesh.shape["seq"]
    nz, side = nb // 2, math.isqrt(ns)
    sizes = {"z": nz, "c": 2, "y": side, "x": side}

    def pairs(axis, k):
        out = []
        if axis in "zc":
            for z in range(nz):
                for c in range(2):
                    to = ((z + k) % nz) * 2 + c if axis == "z" else z * 2 + (c + k) % 2
                    out.append((z * 2 + c, to))
            return "batch", out
        for y in range(side):
            for x in range(side):
                to = ((y + k) % side) * side + x if axis == "y" else y * side + (x + k) % side
                out.append((y * side + x, to))
        return "seq", out

    def push(value, axis, k):
        name, perm = pairs(axis, k)
        return lax.ppermute(value, name, perm)

    def fetch(value, axis, k):
        return push(value, axis, sizes[axis] - k)

    def fetch_plane(value, k, j):
        perm = [
            ((y + k) % side * side + (x + j) % side, y * side + x) for y in range(side) for x in range(side)
        ]
        return lax.ppermute(value, "seq", perm)

    def spread(value, first, second):
        near = jnp.stack([value] + [fetch(value, first, k) for k in range(1, side)])
        return [near] + [fetch(near, second, k) for k in range(1, side)]

    def add(parts):
        return functools.reduce(lambda a, b: a + b, [p.astype(F32) for p in parts])

    def first_half(parts, axis):
        far = [push(parts(k), axis, k) for k in range(1, side)]
        return [parts(0)] + far

    def second_half(mine, axis):
        sent = [push(add([m[j] for m in mine]).astype(BF16), axis, j) for j in range(1, side)]
        return add([m[0] for m in mine] + sent)

    def reduce_z(slots, z):
        got = [push(slots((z + k) % nz).astype(BF16), "z", k) for k in range(1, nz)]
        return add([slots(z)] + got)

    def on_device(tokens, prefix, gain_a, w_q, w_k, w_v, w_o, gain_m, w_gate, w_up, w_down, cot):
        seqs, length, d = tokens.shape
        t = seqs * length
        tokens, cot = tokens.reshape(t, d), cot.reshape(t, d)
        gain_a, gain_m = gain_a[None], gain_m[None]
        bi, si = lax.axis_index("batch"), lax.axis_index("seq")
        z, c, y, x = bi // 2, bi % 2, si // side, si % side
        core = c.astype(jnp.int32)[None]

        def place(k, j):
            return ((y + k) % side) * side + (x + j) % side

        rows, qw, kw = d // nb, d // ns, KV_HEADS * HEAD // ns
        gw = w_gate.shape[1]
        dw = w_down.shape[0]
        ff = gw * ns
        widen = lambda v, lanes: jnp.pad(v, ((0, 0), (0, lanes - v.shape[1])))
        section = ceil_lanes(gw)
        down = w_down.T.reshape(nb // ns, rows, dw)
        down = jnp.concatenate(list(down), 1)
        big = jnp.concatenate(
            [widen(down, section), widen(w_gate, section), widen(w_up, section), widen(w_o, ceil_lanes(qw))], 1
        )
        big = lax.all_gather(big, ("seq", "batch"), axis=0, tiled=True).reshape(ns, d, -1)

        qkv = widen(jnp.concatenate([w_q, w_k, w_v], 1), ceil_lanes(qw + 2 * kw))
        column = jnp.stack([qkv] + [fetch(qkv, "z", k) for k in range(1, nz)])
        plane = [column if k + j == 0 else fetch_plane(column, k, j) for k in range(side) for j in range(side)]
        blocks = plane + [push(v, "c", 1) for v in plane]
        where = [place(k, j) for k in range(side) for j in range(side)]
        where += [((z + k) % nz) * 2 + (c + i) % 2 for i in range(2) for k in range(nz)]
        where = jnp.stack(where).astype(jnp.int32)

        position = si * length + jnp.arange(length, dtype=jnp.int32)
        half = HEAD // 2
        frequency = 10000.0 ** (-(jnp.arange(half, dtype=F32) * 2.0) / (2.0 * half))
        angles = position.astype(F32)[:, None] * frequency[None, :]
        cosine = jnp.tile(jnp.cos(angles), (seqs, 4))
        sine = jnp.sin(angles)
        sine = jnp.tile(jnp.concatenate([-sine, sine], 1), (seqs, 2))
        held = jnp.stack([place(k, j) for k in range(side) for j in range(side)])
        meta = jnp.concatenate([(si * length)[None], held * length, prefix]).astype(jnp.int32)

        cot_t = cot.T
        cot_t2 = push(cot_t, "c", 1)

        w_qkv, na_t, q, k, v = project(tokens, gain_a, cosine, sine, blocks, where, nz)
        w_qkv = w_qkv.reshape(ns, d, -1)
        keys = spread(k, "x", "y")
        values = spread(v, "y", "x")
        mixed, lse = attend(q, keys, values, meta, seqs, length)
        middle, normed_m, nm_t, mix, sq_a = after_attention(mixed, tokens, gain_m, big, nz)
        layer_out, hid, d_gate, d_up, d_middle, d_attn, da_t, gain_m_part, sq_m = feed_forward(
            normed_m, middle, cot, gain_m, big, nb, ff
        )

        def other(v):
            return push(lax.dynamic_index_in_dim(v, 1 - c, 0, False), "c", 1)

        na_t2, nm_t2, mix2 = other(na_t), other(nm_t), other(mix)
        hid2, da_t2 = other(hid), push(da_t, "c", 1)
        d_gate2, d_up2 = push(d_gate, "c", 1), push(d_up, "c", 1)
        d_mixed = mixed_back(d_attn, big)

        y_first = [jnp.stack([place(k, j) for j in range(side)]).astype(jnp.int32) for k in range(side)]
        x_first = [jnp.stack([place(j, k) for j in range(side)]).astype(jnp.int32) for k in range(side)]

        g_do = first_half(
            lambda k: down_out_grads(x_first[k], core, cot_t, cot_t2, hid, hid2, da_t, da_t2, mix, mix2, ns), "x",
        )
        g_gate = first_half(lambda k: row_grads(y_first[k], core, nm_t, nm_t2, d_gate, d_gate2), "y")
        g_up = first_half(lambda k: row_grads(y_first[k], core, nm_t, nm_t2, d_up, d_up2), "y")

        def by_rows(v):
            v = v.astype(BF16).reshape(nz, rows, -1)
            return reduce_z(lambda i: lax.dynamic_index_in_dim(v, i, 0, False), z)

        dqs, k_first, v_first = [], [], []
        for b in range(seqs):
            dq, dk, dv = attend_back(q, keys, values, d_mixed, lse, meta, b, length)
            dqs.append(dq)
            k_first.append(first_half(lambda k: dk[k], "y"))
            v_first.append(first_half(lambda k: dv[k], "x"))
        join = lambda firsts: [jnp.concatenate([f[k] for f in firsts], 1) for k in range(side)]
        dk = second_half(join(k_first), "x")
        dv = second_half(join(v_first), "y")

        g_gate = by_rows(second_half(g_gate, "x"))
        g_up = by_rows(second_half(g_up, "x"))
        do = second_half(g_do, "y").astype(BF16)
        split = nz * dw
        do_d = do[:, :split].reshape(qw, nz, -1)
        do_o = do[:, split:].reshape(qw, nz, -1)
        at = lambda v, i: lax.dynamic_index_in_dim(v, i, 1, False)
        do = reduce_z(lambda i: jnp.concatenate([at(do_d, i), at(do_o, i)], 1), z)

        blk_q, from_q = query_back(dqs, cosine, sine, w_qkv)
        blk_q2 = push(blk_q, "c", 1)
        g_q = first_half(lambda k: row_grads(x_first[k], core, na_t, na_t2, blk_q, blk_q2), "x")
        blk, input_grad, gain_a_part = key_value_back(dk, dv, from_q, cosine, sine, tokens, d_middle, gain_a, w_qkv)
        blk2 = push(blk, "c", 1)
        g_kv = first_half(lambda k: row_grads(y_first[k], core, na_t, na_t2, blk, blk2), "y")
        g_q = by_rows(second_half(g_q, "y"))
        g_kv = by_rows(second_half(g_kv, "x"))

        inputs = tokens.astype(F32)
        sums = jnp.concatenate([gain_a_part, gain_m_part, sq_a, sq_m, jnp.sum(inputs * inputs, 0, keepdims=True)], 0)
        for axis in "cyxz":
            sums = add([sums] + [push(sums, axis, k) for k in range(1, sizes[axis])])
        entries = t * d * nb * ns
        rms = jnp.sqrt(jnp.sum(sums[jnp.array([4, 2, 3])], 1) / entries)
        return (
            layer_out.reshape(seqs, length, d),
            input_grad.reshape(seqs, length, d),
            sums[0],
            g_q[:, :qw],
            g_kv[:, :kw],
            g_kv[:, kw : 2 * kw],
            do[:, dw:].T,
            sums[1],
            g_gate,
            g_up,
            do[:, :dw].T,
            rms,
        )

    rows, flat, copied = P("batch", "seq", None), P("batch", "seq"), P()
    return jax.shard_map(
        on_device,
        mesh=mesh,
        in_specs=(rows, P("batch"), copied, flat, flat, flat, flat, copied, flat, flat, flat, rows),
        out_specs=(rows, rows, copied, flat, flat, flat, flat, copied, flat, flat, flat, copied),
        check_vma=False,
    )
```

```python
import functools
import math

import jax
import jax.numpy as jnp
from jax import lax
from jax.experimental import pallas as pl
from jax.experimental.pallas import tpu as pltpu
from jax.sharding import PartitionSpec as P

HEADS = 18
KV_HEADS = 6
HEAD = 64
SEQ_LEN = 1024
GROUP = HEADS // KV_HEADS
PAIRS = KV_HEADS // 2
EPSILON = 1e-05
MASKED = -1e30
SCALE = HEAD ** (-0.5)
F32 = jnp.float32
BF16 = jnp.bfloat16


def dot(a, b, ca=1, cb=0):
    return lax.dot_general(a, b, (((ca,), (cb,)), ((), ())), preferred_element_type=F32)


def whole(shape, **kw):
    zeros = (0,) * len(shape)
    return pl.BlockSpec(shape, lambda *_: zeros, **kw)


def once(shape):
    return whole(shape, pipeline_mode=pl.Buffered(1))


def call(body, grid, scalars, in_specs, out_specs, out_shape, scratch, args):
    return pl.pallas_call(
        body,
        grid_spec=pltpu.PrefetchScalarGridSpec(
            num_scalar_prefetch=len(scalars),
            grid=grid,
            in_specs=in_specs,
            out_specs=out_specs,
            scratch_shapes=scratch,
        ),
        out_shape=out_shape,
        compiler_params=pltpu.CompilerParams(
            dimension_semantics=("arbitrary",) * len(grid), vmem_limit_bytes=60 * 2**20
        ),
    )(*scalars, *args)


def shape(dims, kind=BF16):
    return jax.ShapeDtypeStruct(dims, kind)


def swap_halves(v):
    lane = lax.broadcasted_iota(jnp.int32, v.shape, 1) % HEAD
    n = v.shape[1]
    return jnp.where(lane < HEAD // 2, pltpu.roll(v, n - HEAD // 2, 1), pltpu.roll(v, HEAD // 2, 1))


def turn(v, cosine, sine):
    width = cosine.shape[1]
    parts = []
    for j in range(v.shape[1] // width):
        u = v[:, j * width : (j + 1) * width]
        parts.append(u * cosine + swap_halves(u) * sine)
    return jnp.concatenate(parts, 1)


def choose(first, pair, own, other):
    a, b = pair
    own[...] = jnp.where(first, a, b)
    other[...] = jnp.where(first, b, a)


def split_rows(value, nz):
    rows = value.shape[0] // (2 * nz)
    take = lambda c: jnp.concatenate(
        [value[(2 * z + c) * rows : (2 * z + c + 1) * rows] for z in range(nz)], 0
    )
    return take(0), take(1)


def split_lanes(value, nz):
    cols = value.shape[1] // (2 * nz)
    take = lambda c: jnp.concatenate(
        [value[:, (2 * z + c) * cols : (2 * z + c + 1) * cols] for z in range(nz)], 1
    )
    return take(0), take(1)


def ceil_lanes(n):
    return -(-n // 128) * 128


def project(tokens, gain, cosine, sine, blocks, where, nz, seqs):
    t, d = tokens.shape
    _, rows, wide = blocks[0].shape
    ns, nb = len(blocks) // 2, 2 * nz
    kv = KV_HEADS * HEAD
    qw, kw = d // ns, kv // ns
    length = t // seqs

    def body(at, tok, gn, cs, sn, *refs):
        parts, outs = refs[: 2 * ns], refs[2 * ns :]
        w, nt, nt2, q = outs[:4]
        pairs, (q_s, k_s, v_s) = outs[4 : 4 + seqs], outs[4 + seqs :]
        for p in range(ns):
            for c in range(2):
                for z in range(nz):
                    w[at[p], at[ns + c * nz + z]] = parts[c * ns + p][z]
        x = tok[...].astype(F32)
        r = lax.rsqrt(jnp.mean(x * x, -1, keepdims=True) + EPSILON)
        n = (x * r * gn[...]).astype(BF16)
        choose(at[ns] % 2 == 0, split_rows(n.T, nz), nt, nt2)
        for i in range(ns):
            weight = jnp.concatenate([w[i, j, :, : qw + 2 * kw] for j in range(nb)], 0)
            y = dot(n, weight)
            q_s[:, i * qw : (i + 1) * qw] = y[:, :qw]
            k_s[:, i * kw : (i + 1) * kw] = y[:, qw : qw + kw]
            v_s[:, i * kw : (i + 1) * kw] = y[:, qw + kw : qw + 2 * kw]
        q[...] = turn(q_s[...], cs[...], sn[...]).astype(BF16)
        key = turn(k_s[...], cs[...], sn[...]).astype(BF16)
        for b in range(seqs):
            rows_b = slice(b * length, (b + 1) * length)
            pairs[b][:, :kv] = key[rows_b]
            pairs[b][:, kv:] = v_s[rows_b, :].astype(BF16)

    return call(
        body,
        (1,),
        (where,),
        [once((t, d)), once((1, d)), once(cosine.shape), once(sine.shape)] + [once(v.shape) for v in blocks],
        [whole((ns, nb, rows, wide)), whole((d // 2, t)), whole((d // 2, t)), whole((t, d))] + [whole((length, 2 * kv))] * seqs,
        [shape((ns, nb, rows, wide)), shape((d // 2, t)), shape((d // 2, t)), shape((t, d))]
        + [shape((length, 2 * kv))] * seqs,
        [pltpu.VMEM((t, d), F32), pltpu.VMEM((t, kv), F32), pltpu.VMEM((t, kv), F32)],
        (tokens, gain, cosine, sine, *blocks),
    )


def fill_bias(meta, bias, ns, length, b):
    prefix = meta[1 + ns + b]
    for i in range(ns):
        key = meta[1 + i] + lax.broadcasted_iota(jnp.int32, (length, length), 0)
        row = meta[0] + lax.broadcasted_iota(jnp.int32, (length, length), 1)
        bias[i * length : (i + 1) * length, :] = jnp.where(
            (key <= row) | (key < prefix), 0.0, MASKED
        ).astype(F32)


def key_rows(refs, lanes):
    return jnp.concatenate([ref[:, lanes] for ref in refs], 0)


def lanes_of(p, width, start=0):
    return pl.ds(pl.multiple_of(start + p * width, 128), width)


def attend(q, held, meta, seq):
    length, pair_width = held[0].shape
    ns, kv, d = len(held), pair_width // 2, q.shape[1]

    def body(meta, qr, *refs):
        kvr, (out, lse, bias) = refs[:ns], refs[ns:]
        fill_bias(meta, bias, ns, length, seq)

        def pair(p, _):
            wide = lanes_of(p, 2 * GROUP * HEAD)
            qp = qr[:, wide]
            kp = key_rows(kvr, lanes_of(p, 2 * HEAD))
            vp = key_rows(kvr, lanes_of(p, 2 * HEAD, kv))
            outs = []
            for g in range(2):
                k = kp[:, g * HEAD : (g + 1) * HEAD]
                vt = vp[:, g * HEAD : (g + 1) * HEAD].T
                for h in range(GROUP):
                    i = g * GROUP + h
                    one = qp[:, i * HEAD : (i + 1) * HEAD] * jnp.asarray(SCALE, BF16)
                    score = dot(k, one, 1, 1) + bias[...]
                    top = jnp.max(score, 0, keepdims=True)
                    e = jnp.exp(score - top)
                    total = jnp.sum(e, 0, keepdims=True)
                    outs.append(dot(vt, e.astype(BF16)) * (1.0 / total))
                    lse[p, pl.ds(i, 1), :] = top + jnp.log(total)
            out[:, wide] = jnp.concatenate(outs, 0).T.astype(BF16)
            return 0

        lax.fori_loop(0, PAIRS, pair, 0)

    return call(
        body,
        (1,),
        (meta,),
        [pl.BlockSpec((length, d), lambda b, m: (seq, 0))] + [whole(v.shape) for v in held],
        [whole((length, d)), whole((PAIRS, 8, length))],
        [shape((length, d)), shape((PAIRS, 8, length), F32)],
        [pltpu.VMEM((SEQ_LEN, length), F32)],
        (q, *held),
    )


def attend_back(q, held, d_mixed, lse, meta, seq):
    length, pair_width = held[0].shape
    ns, kv, d = len(held), pair_width // 2, q.shape[1]

    def body(meta, qr, *refs):
        kvr, (dm, lse, dq), dkv, bias = refs[:ns], refs[ns : ns + 3], refs[ns + 3 : -1], refs[-1]
        fill_bias(meta, bias, ns, length, seq)

        def pair(p, _):
            wide = lanes_of(p, 2 * GROUP * HEAD)
            qp = qr[:, wide]
            dp = dm[:, wide]
            kp = key_rows(kvr, lanes_of(p, 2 * HEAD))
            vp = key_rows(kvr, lanes_of(p, 2 * HEAD, kv))
            dqs, dks, dvs = [], [], []
            for g in range(2):
                k = kp[:, g * HEAD : (g + 1) * HEAD]
                v = vp[:, g * HEAD : (g + 1) * HEAD]
                kt = k.T
                d_key = d_value = None
                for h in range(GROUP):
                    i = g * GROUP + h
                    one = qp[:, i * HEAD : (i + 1) * HEAD] * jnp.asarray(SCALE, BF16)
                    up = dp[:, i * HEAD : (i + 1) * HEAD]
                    score = dot(k, one, 1, 1) + bias[...]
                    w = jnp.exp(score - lse[p, pl.ds(i, 1), :])
                    moved = w * dot(v, up, 1, 1)
                    ds = (moved - w * jnp.sum(moved, 0, keepdims=True)).astype(BF16)
                    dqs.append(dot(kt, ds) * SCALE)
                    a = dot(ds, one)
                    b = dot(w.astype(BF16), up)
                    d_key = a if d_key is None else d_key + a
                    d_value = b if d_value is None else d_value + b
                dks.append(d_key)
                dvs.append(d_value)
            dq[:, wide] = jnp.concatenate(dqs, 0).T
            d_key = jnp.concatenate(dks, 1).astype(BF16)
            d_value = jnp.concatenate(dvs, 1).astype(BF16)
            for i in range(ns):
                rows = slice(i * length, (i + 1) * length)
                dkv[i][:, lanes_of(p, 2 * HEAD)] = d_key[rows]
                dkv[i][:, lanes_of(p, 2 * HEAD, kv)] = d_value[rows]
            return 0

        lax.fori_loop(0, PAIRS, pair, 0)

    row = pl.BlockSpec((length, d), lambda b, m: (seq, 0))
    out = call(
        body,
        (1,),
        (meta,),
        [row] + [whole(v.shape) for v in held] + [row, whole(lse.shape)],
        [whole((length, d))] + [whole(held[0].shape)] * ns,
        [shape((length, d), F32)] + [shape(held[0].shape)] * ns,
        [pltpu.VMEM((SEQ_LEN, length), F32)],
        (q, *held, d_mixed, lse),
    )
    return out[0], out[1:]


def out_section(big, d):
    ns = big.shape[0]
    lanes = ceil_lanes(d // ns)
    return pl.BlockSpec((1, d, lanes), lambda s, *_: (s, 0, big.shape[2] // lanes - 1))


def after_attention(core, mixed, tokens, gain, big, nz):
    t, d = tokens.shape
    n, length = len(mixed), mixed[0].shape[0]
    ns = big.shape[0]
    ow = d // ns

    def body(co, *refs):
        mx, (tok, gn, w, mid, nm, nt, nt2, mc, mc2, sq, acc) = refs[:n], refs[n:]
        s = pl.program_id(0)

        @pl.when(s == 0)
        def _():
            for b in range(n):
                rows = slice(b * length, (b + 1) * length)
                choose(co[0] == 0, split_lanes(mx[b][...], nz), mc.at[rows], mc2.at[rows])

        weight = w[0][:, :ow]
        y = jnp.concatenate([dot(m[...], weight) for m in mx], 0)
        for i in range(ns):

            @pl.when(s == i)
            def _():
                acc[:, i * ow : (i + 1) * ow] = y

        @pl.when(s == ns - 1)
        def _():
            branch = acc[...]
            m = tok[...].astype(F32) + branch
            mid[...] = m
            sq[...] = jnp.sum(branch * branch, 0, keepdims=True)
            r = lax.rsqrt(jnp.mean(m * m, -1, keepdims=True) + EPSILON)
            v = (m * r * gn[...]).astype(BF16)
            nm[...] = v
            choose(co[0] == 0, split_rows(v.T, nz), nt, nt2)

    return call(
        body,
        (ns,),
        (core,),
        [once((length, d))] * n + [once((t, d)), once((1, d)), out_section(big, d)],
        [whole((t, d)), whole((t, d)), whole((d // 2, t)), whole((d // 2, t)),
         whole((t, d // 2)), whole((t, d // 2)), whole((1, d))],
        [shape((t, d), F32), shape((t, d)), shape((d // 2, t)), shape((d // 2, t)),
         shape((t, d // 2)), shape((t, d // 2)), shape((1, d), F32)],
        [pltpu.VMEM((t, d), F32)],
        (*mixed, tokens, gain, big),
    )


def feed_forward(core, normed, middle, cotangent, gain, big, nb, ff):
    t, d = normed.shape
    ns = big.shape[0]
    ratio, width, rows = nb // ns, ff // nb, d // nb
    section = ceil_lanes(ff // ns)
    lanes = width if ratio > 1 else section
    steps = nb

    def body(co, nm, mid, cot, gn, g_w, u_w, d_w, out, hid, hid2, dg, du, dmid, datt, datt_t, gg, sq, acc, dn):
        j = pl.program_id(0)
        n, c = nm[...], cot[...]
        gw_, uw_ = g_w[0][:, :width], u_w[0][:, :width]
        dw_ = jnp.concatenate(
            [d_w[s, :, i * width : (i + 1) * width] for s in range(ns) for i in range(ratio)], 0
        )
        g = dot(n, gw_)
        u = dot(n, uw_)
        dh = dot(c, dw_)
        sg = 1.0 / (1.0 + jnp.exp(-g))
        silu = g * sg
        h = (silu * u).astype(BF16)
        d_gate = (dh * u * sg * (1.0 + g * (1.0 - sg))).astype(BF16)
        d_up = (dh * silu).astype(BF16)

        @pl.when(j % 2 == co[0])
        def _():
            hid[0] = h

        @pl.when(j % 2 != co[0])
        def _():
            hid2[0] = h

        dg[0] = d_gate
        du[0] = d_up
        a = dot(h, dw_, 1, 1)
        b = dot(d_gate, gw_, 1, 1) + dot(d_up, uw_, 1, 1)

        @pl.when(j == 0)
        def _():
            acc[...] = a
            dn[...] = b

        @pl.when(j > 0)
        def _():
            acc[...] += a
            dn[...] += b

        @pl.when(j == steps - 1)
        def _():
            m = mid[...]
            branch = acc[...]
            out[...] = (m + branch).astype(BF16)
            sq[...] = jnp.sum(branch * branch, 0, keepdims=True)
            r = lax.rsqrt(jnp.mean(m * m, -1, keepdims=True) + EPSILON)
            up_ = dn[...]
            gg[...] = jnp.sum(up_ * (m * r), 0, keepdims=True)
            scaled = up_ * gn[...]
            inner = jnp.sum(scaled * m, -1, keepdims=True)
            back = c.astype(F32) + r * scaled - m * (r * r * r * inner * (1.0 / d))
            dmid[...] = back
            low = back.astype(BF16)
            datt[...] = low
            datt_t[...] = low.T

    return call(
        body,
        (steps,),
        (core,),
        [once((t, d)), once((t, d)), once((t, d)), once((1, d)),
         pl.BlockSpec((1, d, lanes), lambda j, co: (j // ratio, 0, section // lanes + j % ratio)),
         pl.BlockSpec((1, d, lanes), lambda j, co: (j // ratio, 0, 2 * section // lanes + j % ratio)),
         pl.BlockSpec((ns, rows, section), lambda j, co: (0, j, 0))],
        [whole((t, d)),
         pl.BlockSpec((1, t, width), lambda j, co: (j // 2, 0, 0)),
         pl.BlockSpec((1, t, width), lambda j, co: (j // 2, 0, 0)),
         pl.BlockSpec((1, t, width), lambda j, co: (j // ratio, 0, j % ratio)),
         pl.BlockSpec((1, t, width), lambda j, co: (j // ratio, 0, j % ratio)),
         whole((t, d)), whole((t, d)), whole((d, t)), whole((1, d)), whole((1, d))],
        [shape((t, d)), shape((nb // 2, t, width)), shape((nb // 2, t, width)), shape((ns, t, ff // ns)), shape((ns, t, ff // ns)),
         shape((t, d), F32), shape((t, d)), shape((d, t)), shape((1, d), F32), shape((1, d), F32)],
        [pltpu.VMEM((t, d), F32), pltpu.VMEM((t, d), F32)],
        (normed, middle, cotangent, gain, big, big, big),
    )


def mixed_back(d_attn, big):
    t, d = d_attn.shape
    ns = big.shape[0]
    ow = d // ns

    def body(da, w, out, acc):
        s = pl.program_id(0)
        weight = w[0][:, :ow]
        for i in range(ns):

            @pl.when(s == i)
            def _():
                y = dot(da[:, i * ow : (i + 1) * ow], weight, 1, 1)
                acc[...] = y if i == 0 else acc[...] + y

        @pl.when(s == ns - 1)
        def _():
            out[...] = acc[...].astype(BF16)

    return call(
        body,
        (ns,),
        (),
        [once((t, d)), out_section(big, d)],
        whole((t, d)),
        shape((t, d)),
        [pltpu.VMEM((t, d), F32)],
        (d_attn, big),
    )


def query_blocks(dqs, cosine, sine, ns):
    length, d = dqs[0].shape
    n = len(dqs)
    qw = d // ns
    pad = ceil_lanes(qw)

    def body(*refs):
        cs, sn, blk = refs[n:]
        for b in range(n):
            rows = slice(b * length, (b + 1) * length)
            v = turn(refs[b][...], cs[rows, :], -sn[rows, :]).astype(BF16)
            for i in range(ns):
                blk[i, rows, :qw] = v[:, i * qw : (i + 1) * qw]
                if pad > qw:
                    blk[i, rows, qw:] = jnp.zeros((length, pad - qw), BF16)

    dims = (ns, n * length, pad)
    return call(
        body, (1,), (), [whole((length, d))] * n + [whole(cosine.shape), whole(sine.shape)],
        whole(dims), shape(dims), [], (*dqs, cosine, sine),
    )


def key_value_blocks(parts, cosine, sine, ns):
    length, pair_width = parts[0][0].shape
    n, kv = len(parts), pair_width // 2
    kw = kv // ns
    pad = ceil_lanes(2 * kw)

    def body(*refs):
        cs, sn, blk = refs[-3:]
        for b in range(n):
            rows = slice(b * length, (b + 1) * length)
            got = refs[b * ns : (b + 1) * ns]
            v = functools.reduce(lambda x, y: x + y, [g[...].astype(F32) for g in got])
            key = turn(v[:, :kv], cs[rows, :], -sn[rows, :]).astype(BF16)
            value = v[:, kv:].astype(BF16)
            for i in range(ns):
                blk[i, rows, :kw] = key[:, i * kw : (i + 1) * kw]
                blk[i, rows, kw : 2 * kw] = value[:, i * kw : (i + 1) * kw]
                if pad > 2 * kw:
                    blk[i, rows, 2 * kw :] = jnp.zeros((length, pad - 2 * kw), BF16)

    dims = (ns, n * length, pad)
    args = [v for group in parts for v in group]
    return call(
        body, (1,), (), [whole(v.shape) for v in args] + [whole(cosine.shape), whole(sine.shape)],
        whole(dims), shape(dims), [], (*args, cosine, sine),
    )


def input_back(blk_q, blk_kv, tokens, d_middle, gain, att):
    t, d = tokens.shape
    ns, _, wide = att.shape
    qw, kw = d // ns, KV_HEADS * HEAD // ns

    def body(bq, bkv, tok, dmid, gn, w, out, gg, acc):
        s = pl.program_id(0)
        y = dot(bq[0][:, :qw], w[0][:, :qw], 1, 1) + dot(bkv[0][:, : 2 * kw], w[0][:, qw : qw + 2 * kw], 1, 1)

        @pl.when(s == 0)
        def _():
            acc[...] = y

        @pl.when(s > 0)
        def _():
            acc[...] += y

        @pl.when(s == ns - 1)
        def _():
            x = tok[...].astype(F32)
            r = lax.rsqrt(jnp.mean(x * x, -1, keepdims=True) + EPSILON)
            up_ = acc[...]
            gg[...] = jnp.sum(up_ * (x * r), 0, keepdims=True)
            scaled = up_ * gn[...]
            inner = jnp.sum(scaled * x, -1, keepdims=True)
            out[...] = dmid[...] + r * scaled - x * (r * r * r * inner * (1.0 / d))

    return call(
        body,
        (ns,),
        (),
        [pl.BlockSpec((1,) + blk_q.shape[1:], lambda s: (s, 0, 0)),
         pl.BlockSpec((1,) + blk_kv.shape[1:], lambda s: (s, 0, 0)),
         once((t, d)), once((t, d)), once((1, d)), pl.BlockSpec((1, d, wide), lambda s: (s, 0, 0))],
        [whole((t, d)), whole((1, d))],
        [shape((t, d), F32), shape((1, d), F32)],
        [pltpu.VMEM((t, d), F32)],
        (blk_q, blk_kv, tokens, d_middle, gain, att),
    )


def row_grads(picks, n_t, n_t2, blk, blk2):
    r, t = n_t.shape
    w = blk.shape[2]
    m = picks.shape[0]

    def body(pk, a, a2, g, g2, out):
        out[0] = (dot(a[...], g[0]) + dot(a2[...], g2[0])).astype(BF16)

    col = pl.BlockSpec((1, t, w), lambda i, pk: (pk[i], 0, 0))
    return call(
        body,
        (m,),
        (picks,),
        [whole((r, t)), whole((r, t)), col, col],
        pl.BlockSpec((1, r, w), lambda i, pk: (i, 0, 0)),
        shape((m, r, w)),
        [],
        (n_t, n_t2, blk, blk2),
    )


def down_out_grads(picks, cot_t, cot_t2, hid, hid2, da_t, da_t2, mix, mix2, ns):
    d, t = cot_t.shape
    w = d // ns
    nz, hw, mw = hid.shape[0], hid.shape[2], mix.shape[1]
    m = picks.shape[0]

    def body(pk, c, c2, h, h2, a, a2, x, x2, out):
        for z in range(nz):
            out[0, :, z * hw : (z + 1) * hw] = (dot(c[...], h[z]) + dot(c2[...], h2[z])).astype(BF16)
        out[0, :, nz * hw :] = (dot(a[...], x[...]) + dot(a2[...], x2[...])).astype(BF16)

    row = pl.BlockSpec((w, t), lambda i, pk: (pk[i], 0))
    return call(
        body,
        (m,),
        (picks,),
        [row, row, whole((nz, t, hw)), whole((nz, t, hw)),
         row, row, whole((t, mw)), whole((t, mw))],
        pl.BlockSpec((1, w, nz * hw + mw), lambda i, pk: (i, 0, 0)),
        shape((m, w, nz * hw + mw)),
        [],
        (cot_t, cot_t2, hid, hid2, da_t, da_t2, mix, mix2),
    )


def solution(mesh):
    nb, ns = mesh.shape["batch"], mesh.shape["seq"]
    nz, side = nb // 2, math.isqrt(ns)
    sizes = {"z": nz, "c": 2, "y": side, "x": side}

    def pairs(axis, k):
        out = []
        if axis in "zc":
            for z in range(nz):
                for c in range(2):
                    to = ((z + k) % nz) * 2 + c if axis == "z" else z * 2 + (c + k) % 2
                    out.append((z * 2 + c, to))
            return "batch", out
        for y in range(side):
            for x in range(side):
                to = ((y + k) % side) * side + x if axis == "y" else y * side + (x + k) % side
                out.append((y * side + x, to))
        return "seq", out

    def push(value, axis, k):
        name, perm = pairs(axis, k)
        return lax.ppermute(value, name, perm)

    around = [(k, j) for k in range(side) for j in range(side)]

    def push_plane(value, k, j):
        perm = [
            (y * side + x, (y + k) % side * side + (x + j) % side) for y in range(side) for x in range(side)
        ]
        return lax.ppermute(value, "seq", perm)

    def fetch_plane(value, k, j):
        return push_plane(value, side - k, side - j)

    def fetch(value, axis, k):
        return push(value, axis, sizes[axis] - k)

    def spread(value, order):
        near = [value] + [fetch(value, order[0], k) for k in range(1, side)]
        packed = jnp.stack(near)
        far = [fetch(packed, order[1], k) for k in range(1, side)]
        of = lambda i, j: near[i] if j == 0 else far[j - 1][i]
        return [of(k, j) if order == "yx" else of(j, k) for k, j in around]

    def after(value, *anchors):
        return lax.optimization_barrier((value, *anchors))[0]

    def add(parts):
        return functools.reduce(lambda a, b: a + b, [p.astype(F32) for p in parts])

    def first_half(parts, axis):
        far = [push(parts(k), axis, k) for k in range(1, side)]
        return [parts(0)] + far

    def second_half(mine, axis):
        sums = [add([m[j] for m in mine]).astype(BF16) for j in range(1, side)]
        sent = [push(v, axis, j) for j, v in enumerate(sums, 1)]

        def rest():
            return add([m[0] for m in mine] + sent).astype(BF16)

        return rest

    def reduce_z(slots, z):
        got = [push(slots((z + k) % nz).astype(BF16), "z", k) for k in range(1, nz)]

        def end():
            return add([slots(z)] + got)

        return end

    def on_device(tokens, prefix, gain_a, w_q, w_k, w_v, w_o, gain_m, w_gate, w_up, w_down, cot):
        seqs, length, d = tokens.shape
        t = seqs * length
        tokens, cot = tokens.reshape(t, d), cot.reshape(t, d)
        gain_a, gain_m = gain_a[None], gain_m[None]
        bi, si = lax.axis_index("batch"), lax.axis_index("seq")
        z, c, y, x = bi // 2, bi % 2, si // side, si % side
        core = c.astype(jnp.int32)[None]

        def place(k, j):
            return ((y + k) % side) * side + (x + j) % side

        rows, qw, kw = d // nb, d // ns, KV_HEADS * HEAD // ns
        gw = w_gate.shape[1]
        dw = w_down.shape[0]
        ff = gw * ns
        widen = lambda v, lanes: jnp.pad(v, ((0, 0), (0, lanes - v.shape[1])))
        section = ceil_lanes(gw)
        down = w_down.T.reshape(nb // ns, rows, dw)
        down = jnp.concatenate(list(down), 1)
        big = jnp.concatenate(
            [widen(down, section), widen(w_gate, section), widen(w_up, section), widen(w_o, ceil_lanes(qw))], 1
        )
        big = lax.all_gather(big, ("seq", "batch"), axis=0, tiled=True).reshape(ns, d, -1)

        att = widen(jnp.concatenate([w_q, w_k, w_v], 1), ceil_lanes(qw + 2 * kw))
        column = jnp.stack([att] + [fetch(att, "z", k) for k in range(1, nz)])
        plane = [column] + [fetch_plane(column, k, j) for k, j in around[1:]]
        blocks = plane + [push(v, "c", 1) for v in plane]
        where = [place(k, j) for k, j in around]
        where += [((z + k) % nz) * 2 + (c + i) % 2 for i in range(2) for k in range(nz)]
        where = jnp.stack(where).astype(jnp.int32)

        position = si * length + jnp.arange(length, dtype=jnp.int32)
        half = HEAD // 2
        frequency = 10000.0 ** (-(jnp.arange(half, dtype=F32) * 2.0) / (2.0 * half))
        angles = position.astype(F32)[:, None] * frequency[None, :]
        cosine = jnp.tile(jnp.cos(angles), (seqs, 4))
        sine = jnp.sin(angles)
        sine = jnp.tile(jnp.concatenate([-sine, sine], 1), (seqs, 2))
        held = jnp.stack([place(k, j) for k, j in around])
        meta = jnp.concatenate([(si * length)[None], held * length, prefix]).astype(jnp.int32)

        cot_t = cot.T
        cot_t2 = push(cot_t, "c", 1)

        w_att, na_t, na_far, q, *pairs_kv = project(tokens, gain_a, cosine, sine, blocks, where, nz, seqs)
        w_att = w_att.reshape(ns, d, -1)
        rows_kv = [spread(v, "xy" if b % 2 else "yx") for b, v in enumerate(pairs_kv)]
        mixed, lse = zip(*[attend(q, v, meta, b) for b, v in enumerate(rows_kv)])
        middle, normed_m, nm_t, nm_far, mix, mix_far, sq_a = after_attention(
            core, mixed, tokens, gain_m, big, nz)
        layer_out, hid, hid_far, d_gate, d_up, d_middle, d_attn, da_t, gain_m_part, sq_m = feed_forward(
            core, normed_m, middle, cot, gain_m, big, nb, ff
        )
        na_t2, nm_t2 = push(na_far, "c", 1), push(nm_far, "c", 1)
        mix2, hid2 = push(mix_far, "c", 1), push(hid_far, "c", 1)
        da_t2 = push(da_t, "c", 1)
        d_gate2, d_up2 = push(d_gate, "c", 1), push(d_up, "c", 1)
        d_mixed = mixed_back(d_attn, big)

        y_first = [jnp.stack([place(k, j) for j in range(side)]).astype(jnp.int32) for k in range(side)]
        x_first = [jnp.stack([place(j, k) for j in range(side)]).astype(jnp.int32) for k in range(side)]

        g_do = first_half(
            lambda k: down_out_grads(x_first[k], cot_t, cot_t2, hid, hid2, da_t, da_t2, mix, mix2, ns), "x",
        )
        g_gate = first_half(lambda k: row_grads(y_first[k], nm_t, nm_t2, d_gate, d_gate2), "y")
        g_up = first_half(lambda k: row_grads(x_first[k], nm_t, nm_t2, d_up, d_up2), "x")

        def by_rows(v):
            v = v.astype(BF16).reshape(nz, rows, -1)
            return reduce_z(lambda i: lax.dynamic_index_in_dim(v, i, 0, False), z)

        d_mixed = after(d_mixed, g_do[0], g_gate[0], g_up[0])
        dqs, parts = [], []
        for b in range(seqs):
            dq, dkv = attend_back(q, rows_kv[b], d_mixed, lse[b], meta, b)
            dqs.append(dq)
            parts.append([dkv[0]] + [push_plane(v, k, j) for v, (k, j) in zip(dkv[1:], around[1:])])

        g_gate = by_rows(second_half(g_gate, "x")())
        g_up = by_rows(second_half(g_up, "y")())
        do = second_half(g_do, "y")().astype(BF16)
        split = nz * dw
        do_d = do[:, :split].reshape(qw, nz, -1)
        do_o = do[:, split:].reshape(qw, nz, -1)
        at = lambda v, i: lax.dynamic_index_in_dim(v, i, 1, False)
        do = reduce_z(lambda i: jnp.concatenate([at(do_d, i), at(do_o, i)], 1), z)

        blk_q = query_blocks(dqs, cosine, sine, ns)
        blk_q2 = push(blk_q, "c", 1)
        g_q = first_half(lambda k: row_grads(y_first[k], na_t, na_t2, blk_q, blk_q2), "y")
        blk = key_value_blocks(parts, cosine, sine, ns)
        blk2 = push(blk, "c", 1)
        g_kv = first_half(lambda k: row_grads(y_first[k], na_t, na_t2, blk, blk2), "y")
        d_middle = after(d_middle, g_kv[0])
        input_grad, gain_a_part = input_back(blk_q, blk, tokens, d_middle, gain_a, w_att)
        late = lambda parts: [parts[0]] + [after(v, gain_a_part) for v in parts[1:]]
        kv_rest = second_half(late(g_kv), "x")
        q_rest = second_half(late(g_q), "x")

        inputs = tokens.astype(F32)
        sums = jnp.concatenate([gain_a_part, gain_m_part, sq_a, sq_m, jnp.sum(inputs * inputs, 0, keepdims=True)], 0)
        sums = sums + push(sums, "c", 1)
        do, g_gate, g_up = [f() for f in (do, g_gate, g_up)]
        near = [push_plane(sums, k, j) for k, j in around[1:]]
        g_kv = by_rows(kv_rest())
        g_q = by_rows(q_rest())
        sums = add([sums] + near)
        sums = add([sums] + [push(sums, "z", k) for k in range(1, nz)])
        g_q, g_kv = g_q(), g_kv()
        entries = t * d * nb * ns
        rms = jnp.sqrt(jnp.sum(sums[jnp.array([4, 2, 3])], 1) / entries)
        return (
            layer_out.reshape(seqs, length, d),
            input_grad.reshape(seqs, length, d),
            sums[0],
            g_q[:, :qw],
            g_kv[:, :kw],
            g_kv[:, kw : 2 * kw],
            do[:, dw:].T,
            sums[1],
            g_gate,
            g_up,
            do[:, :dw].T,
            rms,
        )

    rows, flat, copied = P("batch", "seq", None), P("batch", "seq"), P()
    return jax.shard_map(
        on_device,
        mesh=mesh,
        in_specs=(rows, P("batch"), copied, flat, flat, flat, flat, copied, flat, flat, flat, rows),
        out_specs=(rows, rows, copied, flat, flat, flat, flat, copied, flat, flat, flat, copied),
        check_vma=False,
    )
```
